128 devices in a mesh: section: 8 (over x, core), mat: 16 (over y, z).
Axes of the slice: x: 4, y: 4, z: 4, core: 2. Of those that a mesh axis runs over, the one named last changes fastest.
Arguments:
- eigvec: bfloat16 [8, 3072, 3072], P('section')
- eig_level: float32 [8, 3072], P('section'), may hold values from 0.5 to 5
- energies: float32 [2], replicated, may hold values from -0.3 to 0.45
- order: int32 [2], replicated, may hold values from 0 to 1, each once
- init_r: bfloat16 [2, 3072, 3072], P(None, 'mat')
Outputs:
- boundary_r: bfloat16 [8, 2, 3072, 3072], P('section', None, 'mat')
The draws below stay inside these ranges and needn't reach their ends.
Inputs may be any that keep to these rules, and one draw needn't show every extreme that they name: order holds each of 0 to 1 once.
All inputs are finite; a program needn't handle non-finite values.
Results may differ from the reference program's by a relative error of at most 0.0064.
Values may be sent and summed in bfloat16 or wider, within the bound.
A program may use at most 128 MiB of HBM per device.

```python
import math
import jax
import jax.numpy as jnp
from jax import lax

NCH = 3072
SECTORS = 8
ENERGIES = 2


def draw_eigvec(key, part):
    half = NCH // 2
    angles = jax.random.uniform(jax.random.fold_in(key, 31), (SECTORS, half), jnp.float32, -0.8, 0.8)
    angle_full = jnp.concatenate([angles, angles], axis=1)
    sign_full = jnp.concatenate([jnp.ones((half,), jnp.float32), -jnp.ones((half,), jnp.float32)])
    rows = lax.broadcasted_iota(jnp.int32, (NCH, NCH), 0)
    cols = lax.broadcasted_iota(jnp.int32, (NCH, NCH), 1)
    partner = (cols + half) % NCH
    on_diag = (rows == cols).astype(jnp.float32)
    on_pair = (rows == partner).astype(jnp.float32)
    cosine = jnp.cos(angle_full)[:, None, :]
    sine = (sign_full[None, :] * jnp.sin(angle_full))[:, None, :]
    rotation = on_diag[None] * cosine + on_pair[None] * sine
    mixing = jax.random.normal(jax.random.fold_in(key, 32), (SECTORS, NCH, NCH), jnp.float32)
    return (rotation + 0.35 / math.sqrt(NCH) * mixing).astype(jnp.bfloat16)


def draw_eig_level(key, part):
    return jnp.exp(jax.random.uniform(jax.random.fold_in(key, 44), (SECTORS, NCH), jnp.float32, math.log(0.5), math.log(5.0)))


def draw_energies(key, part):
    return jax.random.uniform(jax.random.fold_in(key, 52), (ENERGIES,), jnp.float32, -0.3, 0.45)


def draw_init_r(key, part):
    normal_part = jax.random.normal(jax.random.fold_in(key, 11), (ENERGIES, NCH, NCH), jnp.float32)
    symmetric = (normal_part + jnp.swapaxes(normal_part, 1, 2)) * (0.4 / math.sqrt(NCH))
    levels = jax.random.uniform(jax.random.fold_in(key, 12), (ENERGIES, NCH), jnp.float32, 0.5, 2.5)
    identity = jnp.eye(NCH, dtype=jnp.float32)
    return (symmetric + levels[:, :, None] * identity[None]).astype(jnp.bfloat16)


def setup_inputs(seed: int = 0) -> dict:
    splits = jax.random.split(jax.random.key(seed), 6)
    return {
        "eigvec": draw_eigvec(jax.random.fold_in(splits[5], 71), 0),
        "eig_level": draw_eig_level(jax.random.fold_in(splits[5], 71), 0),
        "energies": draw_energies(jax.random.fold_in(splits[5], 71), 0),
        "order": jax.random.permutation(splits[3], ENERGIES).astype(jnp.int32),
        "init_r": draw_init_r(jax.random.fold_in(splits[5], 71), 0),
    }


sector_width = 1.0

def greens(levels, energy):
    wave_number = jnp.sqrt(levels - energy)
    phase_arg = wave_number * sector_width
    sinh_value = jnp.sinh(phase_arg)
    g_one = jnp.cosh(phase_arg) / (wave_number * sinh_value)
    g_two = 1.0 / (wave_number * sinh_value)
    return (g_one, g_two)

def propagate(r_inner, g_one, g_two):
    precond = 1.0 / (g_one + jnp.abs(jnp.diagonal(r_inner)))
    side = g_two * precond
    diag_term = g_one - 2.0 * g_two * g_two * precond + g_one * side * side
    return side[:, None] * r_inner * side[None, :] + jnp.diag(diag_term)

def chain(eigvec, eig_level, energy, r_now):
    results = []
    for sector in range(SECTORS):
        sector_vecs = eigvec[sector]
        g_one, g_two = greens(eig_level[sector], energy)
        half_left = jnp.dot(r_now, sector_vecs, preferred_element_type=jnp.float32).astype(jnp.bfloat16)
        r_inner = jnp.dot(half_left.T, sector_vecs, preferred_element_type=jnp.float32)
        r_outer = propagate(r_inner, g_one, g_two).astype(jnp.bfloat16)
        half_right = jnp.dot(r_outer, sector_vecs.T, preferred_element_type=jnp.float32).astype(jnp.bfloat16)
        r_now = jnp.dot(half_right.T, sector_vecs.T, preferred_element_type=jnp.float32).astype(jnp.bfloat16)
        results.append(r_now)
    return jnp.stack(results)

def reference(eigvec, eig_level, energies, order, init_r):

    def one_slot(slot):
        picked = order[slot]
        return chain(eigvec, eig_level, energies[picked], init_r[picked])
    stacked = lax.map(one_slot, jnp.arange(ENERGIES, dtype=jnp.int32))
    return jnp.swapaxes(stacked, 0, 1)
```

```python
import functools

import jax
import jax.numpy as jnp
from jax import lax
from jax.experimental import pallas as pl
from jax.experimental.pallas import tpu as pltpu
from jax.sharding import PartitionSpec as P

MESH = pl.DeviceIdType.MESH
SIDE = 4
MATS = SIDE * SIDE
MAIN = 128
sector_width = 1.0


def greens(levels, energy):
    wave_number = jnp.sqrt(levels - energy)
    phase_arg = wave_number * sector_width
    sinh_value = jnp.sinh(phase_arg)
    g_one = jnp.cosh(phase_arg) / (wave_number * sinh_value)
    g_two = 1.0 / (wave_number * sinh_value)
    return (g_one, g_two)


def kernel(
    sections,
    eig_ref, g_one_ref, g_two_ref, init_ref, out_ref,
    vecs, vecs_t, rmat, inner, outer, half_lhs, send, recv, diag_send, diag_recv, side_ref,
    load_sem, init_sem, out_sem, send_sem, recv_sem, diag_send_sem, diag_recv_sem,
    pass_send_sem, pass_recv_sem,
):
    nch = vecs.shape[0]
    rows = rmat.shape[1]
    rest = rows - MAIN
    tall = rows // 2
    half = nch // 2
    tile = rows * SIDE
    win = 2 * rows
    f32, bf16 = jnp.float32, jnp.bfloat16

    section = lax.axis_index("section")
    me = lax.axis_index("mat")
    y, z = me // SIDE, me % SIDE
    odd = me % 2
    y_order = [(y + 2) % SIDE, SIDE - 1 - y, y + 1 - 2 * (y % 2), y]
    own_half = y // 2
    far_half = 1 - own_half

    def load(h):
        part = pl.ds(h * half, half)
        return pltpu.make_async_copy(eig_ref.at[0, part], vecs.at[part], load_sem.at[h])

    for h in range(2):
        load(h).start()

    def row_copies(slot):
        first = pl.multiple_of(odd * rest, rest)
        second = pl.multiple_of(MAIN * (1 - odd), rest)
        return ((pl.ds(first, MAIN), pl.ds(0, MAIN)), (pl.ds(second, rest), pl.ds(MAIN, rest)))

    def init_copies(slot):
        return [
            pltpu.make_async_copy(init_ref.at[slot, a], rmat.at[slot, b], init_sem.at[slot, n])
            for n, (a, b) in enumerate(row_copies(slot))
        ]

    def out_copies(slot):
        return [
            pltpu.make_async_copy(rmat.at[slot, b], out_ref.at[0, slot, a], out_sem.at[slot, n])
            for n, (a, b) in enumerate(row_copies(slot))
        ]

    @pl.when(section == 0)
    def _():
        for slot in range(2):
            for copy in init_copies(slot):
                copy.start()

    barrier = pltpu.get_barrier_semaphore()

    @pl.loop(0, MATS)
    def _(peer):
        @pl.when(peer != me)
        def _():
            pl.semaphore_signal(barrier, inc=1, device_id=(section, peer), device_id_type=MESH)

    @pl.when(section > 0)
    def _():
        pl.semaphore_signal(barrier, inc=1, device_id=(section - 1, me), device_id_type=MESH)

    @pl.when(section < sections - 1)
    def _():
        pl.semaphore_signal(barrier, inc=1, device_id=(section + 1, me), device_id_type=MESH)

    has_last = (section + sections - 1) // sections
    has_next = (2 * sections - 2 - section) // sections
    pl.semaphore_wait(barrier, MATS - 1 + has_last + has_next)

    lane = lax.broadcasted_iota(jnp.int32, (tall, MAIN), 1)
    low = lane < rest
    row_id = lax.broadcasted_iota(jnp.int32, (rows, win), 0)
    col_id = lax.broadcasted_iota(jnp.int32, (rows, win), 1)
    target = jnp.where(odd == 0, row_id, jnp.where(row_id < MAIN, row_id + win - MAIN, row_id + rest))
    on_diag = col_id == target
    win_cols = pl.ds(pl.multiple_of((me // 2) * win, MAIN), win)

    def transpose_vecs():
        @pl.loop(0, nch // MAIN)
        def _(r):
            part = pl.ds(pl.multiple_of(r * MAIN, MAIN), MAIN)
            vecs_t[:, part] = vecs[part, :].T

    def block_copy(trip, slot, place, dest):
        return pltpu.make_async_remote_copy(
            src_ref=send.at[slot, place],
            dst_ref=recv.at[trip, slot, me],
            send_sem=send_sem.at[slot, place],
            recv_sem=recv_sem.at[trip, slot, me],
            device_id=(section, dest),
            device_id_type=MESH,
        )

    def block_arrival(trip, slot, source):
        return pltpu.make_async_remote_copy(
            src_ref=send.at[slot, 0],
            dst_ref=recv.at[trip, slot, source],
            send_sem=send_sem.at[slot, 0],
            recv_sem=recv_sem.at[trip, slot, source],
            device_id=(section, source),
            device_id_type=MESH,
        )

    def ship(trip, slot, step, value):
        main_t = value[:MAIN].T
        rest_t = value[rest:].T
        for j in range(SIDE):
            base = rows * j
            if j % 2 == 0:
                main = main_t[base:base + rows]
                top = rest_t[base:base + tall]
                bottom = rest_t[base + tall:base + rows]
            else:
                main = jnp.concatenate([main_t[base + rest:base + rows], main_t[base:base + rest]], 0)
                top = rest_t[base + rest:base + rest + tall]
                bottom = jnp.concatenate([rest_t[base + rest + tall:base + rows], rest_t[base:base + rest]], 0)
            packed = jnp.where(low, pltpu.roll(top, rest, 1), bottom)
            place = SIDE * step + j
            send[slot, place, :rows] = main.astype(bf16)
            send[slot, place, rows:] = packed.astype(bf16)
        for j in range(SIDE):
            place = SIDE * step + j
            dest = y_order[step] * SIDE + j
            if step < SIDE - 1:
                block_copy(trip, slot, place, dest).start()
            else:
                @pl.when(j != z)
                def _():
                    block_copy(trip, slot, place, dest).start()
        if step == SIDE - 1:
            recv[trip, slot, me] = send[slot, SIDE * step + z]

    def wait_sent(trip, slot):
        for place in range(MATS):
            dest = y_order[place // SIDE] * SIDE + place % SIDE
            if place < MATS - SIDE:
                block_copy(trip, slot, place, dest).wait_send()
            else:
                @pl.when(place % SIDE != z)
                def _():
                    block_copy(trip, slot, place, dest).wait_send()

    def gather_half(trip, slot, which, own):
        for n in range(MATS // 2):
            source = which * (MATS // 2) + n
            if own:
                @pl.when(source != me)
                def _():
                    block_arrival(trip, slot, source).wait_recv()
            else:
                block_arrival(trip, slot, source).wait_recv()
        for q in range(MATS // 4):
            even = which * (MATS // 2) + 2 * q
            base = win * q
            half_lhs[:, base:base + MAIN] = recv[trip, slot, even, :rows]
            half_lhs[:, base + 2 * MAIN:base + 3 * MAIN] = recv[trip, slot, even + 1, :rows]
            left = recv[trip, slot, even, rows:].astype(f32)
            right = recv[trip, slot, even + 1, rows:].astype(f32)
            top = jnp.where(low, left, pltpu.roll(right, rest, 1))
            bottom = jnp.where(low, pltpu.roll(left, rest, 1), right)
            half_lhs[:tall, base + MAIN:base + 2 * MAIN] = top.astype(bf16)
            half_lhs[tall:, base + MAIN:base + 2 * MAIN] = bottom.astype(bf16)

    def dot(a, b):
        return jnp.dot(a, b, preferred_element_type=f32)

    def half_rows(which):
        return pl.ds(pl.multiple_of(which * half, MAIN), half)

    def pass_copy(slot, n):
        part = pl.ds(n * tile, tile)
        return pltpu.make_async_remote_copy(
            src_ref=rmat.at[slot, :, part],
            dst_ref=rmat.at[slot, :, part],
            send_sem=pass_send_sem.at[slot, n],
            recv_sem=pass_recv_sem.at[slot, n],
            device_id=(section + 1, me),
            device_id_type=MESH,
        )

    def pass_arrival(slot, n):
        part = pl.ds(n * tile, tile)
        return pltpu.make_async_remote_copy(
            src_ref=rmat.at[slot, :, part],
            dst_ref=rmat.at[slot, :, part],
            send_sem=pass_send_sem.at[slot, n],
            recv_sem=pass_recv_sem.at[slot, n],
            device_id=(section - 1, me),
            device_id_type=MESH,
        )

    def left_half(slot):
        @pl.when(section == 0)
        def _():
            for copy in init_copies(slot):
                copy.wait()

        for h in range(2):
            @pl.when(section > 0)
            def _():
                for n in range(2 * h, 2 * h + 2):
                    pass_arrival(slot, n).wait_recv()

            if h == 0:
                for n in range(2):
                    cols = slice(n * half, (n + 1) * half)
                    inner[slot, :, cols] = dot(rmat[slot, :, :half], vecs[:half, cols])
        for step in range(SIDE):
            cols = pl.ds(pl.multiple_of(y_order[step] * tile, MAIN), tile)
            value = inner[slot, :, cols] + dot(rmat[slot, :, half:], vecs[half:, cols])
            ship(0, slot, step, value)

    def diag_copy(slot, dest):
        return pltpu.make_async_remote_copy(
            src_ref=diag_send.at[slot],
            dst_ref=diag_recv.at[slot, me],
            send_sem=diag_send_sem.at[slot, dest],
            recv_sem=diag_recv_sem.at[slot, me],
            device_id=(section, dest),
            device_id_type=MESH,
        )

    def diag_arrival(slot, source):
        return pltpu.make_async_remote_copy(
            src_ref=diag_send.at[slot],
            dst_ref=diag_recv.at[slot, source],
            send_sem=diag_send_sem.at[slot, source],
            recv_sem=diag_recv_sem.at[slot, source],
            device_id=(section, source),
            device_id_type=MESH,
        )

    def inner_product(slot):
        gather_half(0, slot, far_half, False)
        for n in range(2):
            cols = slice(n * half, (n + 1) * half)
            inner[slot, :, cols] = dot(half_lhs[...], vecs[half_rows(far_half), cols])
        gather_half(0, slot, own_half, True)
        for n in range(2):
            cols = slice(n * half, (n + 1) * half)
            inner[slot, :, cols] += dot(half_lhs[...], vecs[half_rows(own_half), cols])
        mine = jnp.sum(jnp.where(on_diag, inner[slot, :, win_cols], 0.0), axis=0, keepdims=True)
        diag_send[slot] = jnp.zeros(diag_send.shape[1:], f32)
        for n in range(win // MAIN):
            diag_send[slot, n:n + 1, :] = mine[:, n * MAIN:(n + 1) * MAIN]
        diag_recv[slot, me] = diag_send[slot]

        @pl.loop(0, MATS)
        def _(dest):
            @pl.when(dest != me)
            def _():
                diag_copy(slot, dest).start()

    def right_half(slot):
        @pl.loop(0, MATS)
        def _(source):
            @pl.when(source != me)
            def _():
                diag_arrival(slot, source).wait_recv()

        pieces = []
        for p in range(MATS // 2):
            pair = diag_recv[slot, 2 * p] + diag_recv[slot, 2 * p + 1]
            pieces += [pair[n:n + 1, :] for n in range(win // MAIN)]
        full_diag = jnp.concatenate(pieces, axis=1)
        g_one = g_one_ref[slot:slot + 1, :]
        g_two = g_two_ref[slot:slot + 1, :]
        precond = 1.0 / (g_one + jnp.abs(full_diag))
        side = g_two * precond
        term = g_one - 2.0 * g_two * g_two * precond + g_one * side * side
        side_ref[0:1, :] = side
        side_ref[1:2, :] = term
        side_win = side_ref[0:1, win_cols]
        term_win = side_ref[1:2, win_cols]
        side_rows = jnp.sum(jnp.where(on_diag, side_win, 0.0), axis=1, keepdims=True)
        for q in range(nch // win):
            cols = slice(q * win, (q + 1) * win)
            outer[:, cols] = (side_rows * inner[slot, :, cols] * side[:, cols]).astype(bf16)
        scaled = side_rows * inner[slot, :, win_cols] * side_win
        outer[:, win_cols] = (scaled + jnp.where(on_diag, term_win, 0.0)).astype(bf16)
        wait_sent(0, slot)
        for step in range(SIDE):
            cols = pl.ds(pl.multiple_of(y_order[step] * tile, MAIN), tile)
            ship(1, slot, step, dot(outer[...], vecs_t[:, cols]))

    def next_rows(slot):
        gather_half(1, slot, far_half, False)
        for n in range(2):
            cols = slice(n * half, (n + 1) * half)
            inner[slot, :, cols] = dot(half_lhs[...], vecs_t[half_rows(far_half), cols])
        gather_half(1, slot, own_half, True)
        for n in range(SIDE):
            cols = slice(n * tile, (n + 1) * tile)
            value = inner[slot, :, cols] + dot(half_lhs[...], vecs_t[half_rows(own_half), cols])
            rmat[slot, :, cols] = value.astype(bf16)

            @pl.when(section < sections - 1)
            def _():
                pass_copy(slot, n).start()
        for copy in out_copies(slot):
            copy.start()

    for h in range(2):
        load(h).wait()

    @pl.when(section > 0)
    def _():
        transpose_vecs()

    left_half(0)

    @pl.when(section == 0)
    def _():
        transpose_vecs()

    inner_product(0)
    left_half(1)
    right_half(0)
    inner_product(1)
    next_rows(0)
    right_half(1)
    next_rows(1)

    for slot in range(2):
        wait_sent(1, slot)
        for copy in out_copies(slot):
            copy.wait()

        @pl.loop(0, MATS)
        def _(dest):
            @pl.when(dest != me)
            def _():
                diag_copy(slot, dest).wait_send()

        @pl.when(section < sections - 1)
        def _():
            for n in range(SIDE):
                pass_copy(slot, n).wait_send()


def on_device(sections, eigvec, eig_level, energies, order, init_r):
    nch = eigvec.shape[1]
    rows = init_r.shape[1]
    g_one, g_two = greens(eig_level[0][None, :], jnp.take(energies, order)[:, None])
    initial = jnp.take(init_r, order, axis=0)
    any_spec = pl.BlockSpec(memory_space=pl.ANY)
    vmem_spec = pl.BlockSpec(memory_space=pltpu.VMEM)
    dma = pltpu.SemaphoreType.DMA
    bf16, f32 = jnp.bfloat16, jnp.float32
    block = rows + rows // 2
    return pl.pallas_call(
        functools.partial(kernel, sections),
        out_shape=jax.ShapeDtypeStruct((1, 2, rows, nch), bf16),
        in_specs=[any_spec, vmem_spec, vmem_spec, any_spec],
        out_specs=any_spec,
        scratch_shapes=[
            pltpu.VMEM((nch, nch), bf16),
            pltpu.VMEM((nch, nch), bf16),
            pltpu.VMEM((2, rows, nch), bf16),
            pltpu.VMEM((2, rows, nch), f32),
            pltpu.VMEM((rows, nch), bf16),
            pltpu.VMEM((rows, nch // 2), bf16),
            pltpu.VMEM((2, MATS, block, MAIN), bf16),
            pltpu.VMEM((2, 2, MATS, block, MAIN), bf16),
            pltpu.VMEM((2, 8, MAIN), f32),
            pltpu.VMEM((2, MATS, 8, MAIN), f32),
            pltpu.VMEM((2, nch), f32),
            dma((2,)),
            dma((2, 2)),
            dma((2, 2)),
            dma((2, MATS)),
            dma((2, 2, MATS)),
            dma((2, MATS)),
            dma((2, MATS)),
            dma((2, SIDE)),
            dma((2, SIDE)),
        ],
        compiler_params=pltpu.CompilerParams(
            collective_id=0, has_side_effects=True, vmem_limit_bytes=67043328
        ),
        name="sectors",
    )(eigvec, g_one, g_two, initial)


def solution(mesh):
    in_specs = (P("section", None, None), P("section", None), P(), P(), P(None, "mat", None))
    out_specs = P("section", None, "mat", None)
    return jax.shard_map(
        functools.partial(on_device, mesh.shape["section"]),
        mesh=mesh, in_specs=in_specs, out_specs=out_specs, check_vma=False,
    )
```

```python
import functools

import jax
import jax.numpy as jnp
from jax import lax
from jax.experimental import pallas as pl
from jax.experimental.pallas import tpu as pltpu
from jax.sharding import PartitionSpec as P

MESH = pl.DeviceIdType.MESH
SIDE = 4
MATS = SIDE * SIDE
MAIN = 128
sector_width = 1.0


LEFT, INNER, PROPAGATE, RIGHT, NEXT, FLIP_OUT, FLIP_IN, TURN = range(8)
FIRST = [
    (LEFT, 0), (TURN, 0), (INNER, 0), (TURN, 1), (PROPAGATE, 0), (RIGHT, 0), (LEFT, 1),
    (NEXT, 0), (INNER, 1), (PROPAGATE, 1), (RIGHT, 1), (NEXT, 1),
]
CHAIN = [
    (LEFT, 0), (INNER, 0), (PROPAGATE, 0), (LEFT, 1), (INNER, 1), (PROPAGATE, 1),
]
PLAIN = CHAIN + [(RIGHT, 0), (RIGHT, 1), (NEXT, 0), (NEXT, 1)]
FLIPPED = CHAIN + [
    (FLIP_OUT, 0), (FLIP_OUT, 1), (FLIP_IN, 0), (RIGHT, 0), (FLIP_IN, 1), (RIGHT, 1),
    (NEXT, 0), (NEXT, 1),
]
LAST = [
    (LEFT, 0), (INNER, 0), (PROPAGATE, 0), (LEFT, 1), (RIGHT, 0), (INNER, 1), (NEXT, 0),
    (PROPAGATE, 1), (RIGHT, 1), (NEXT, 1),
]
STEPS, BASE, DIGITS = 14, 17, 7


def digits(order):
    codes = [2 * stage + slot for stage, slot in order]
    codes += [BASE - 1] * (STEPS - len(codes))
    return [
        sum(code * BASE ** n for n, code in enumerate(codes[part:part + DIGITS]))
        for part in (0, DIGITS)
    ]


def greens(levels, energy):
    wave_number = jnp.sqrt(levels - energy)
    phase_arg = wave_number * sector_width
    sinh_value = jnp.sinh(phase_arg)
    g_one = jnp.cosh(phase_arg) / (wave_number * sinh_value)
    g_two = 1.0 / (wave_number * sinh_value)
    return (g_one, g_two)


def kernel(
    sections,
    eig_ref, g_one_ref, g_two_ref, init_ref, out_ref,
    vecs, vecs_t, rmat, inner, outer, half_lhs, send, recv, diag_send, diag_recv, side_ref,
    load_sem, init_sem, out_sem, send_sem, recv_sem, diag_send_sem, diag_recv_sem,
    pass_send_sem, pass_recv_sem, slice_send_sem, slice_recv_sem, stream_send_sem, stream_recv_sem,
    ring_send_sem, ring_recv_sem, ready_sem, go_sem,
):
    nch = vecs.shape[0]
    rows = rmat.shape[1]
    rest = rows - MAIN
    tall = rows // 2
    half = nch // 2
    tile = rows * SIDE
    win = 2 * rows
    f32, bf16 = jnp.float32, jnp.bfloat16

    section = lax.axis_index("section")
    me = lax.axis_index("mat")
    y, z = me // SIDE, me % SIDE
    odd = me % 2
    y_order = [(y + 2) % SIDE, SIDE - 1 - y, y + 1 - 2 * (y % 2), y]
    own_half = y // 2
    far_half = 1 - own_half

    even_section = section % 2 == 0
    flipped = even_section & (section >= 2)
    last = sections - 1
    f_dot = functools.partial(jnp.dot, preferred_element_type=f32)

    def load(h, space):
        part = pl.ds(h * half, half)
        return pltpu.make_async_copy(eig_ref.at[0, part], space.at[part], load_sem.at[h])

    def load_too(h):
        part = pl.ds(h * half, half)
        return pltpu.make_async_copy(eig_ref.at[0, part], vecs.at[part], load_sem.at[2 + h])

    @pl.when(even_section)
    def _():
        for h in range(2):
            load(h, vecs).start()

    @pl.when(section % 2 == 1)
    def _():
        for h in range(2):
            load(h, vecs_t).start()

    @pl.when(section == 1)
    def _():
        for h in range(2):
            load_too(h).start()

    def row_copies(slot):
        first = pl.multiple_of(odd * rest, rest)
        second = pl.multiple_of(MAIN * (1 - odd), rest)
        return ((pl.ds(first, MAIN), pl.ds(0, MAIN)), (pl.ds(second, rest), pl.ds(MAIN, rest)))

    def init_copies(slot):
        return [
            pltpu.make_async_copy(init_ref.at[slot, a], rmat.at[slot, b], init_sem.at[slot, n])
            for n, (a, b) in enumerate(row_copies(slot))
        ]

    def out_copies(slot):
        return [
            pltpu.make_async_copy(rmat.at[slot, b], out_ref.at[0, slot, a], out_sem.at[slot, n])
            for n, (a, b) in enumerate(row_copies(slot))
        ]

    @pl.when(section == 0)
    def _():
        for slot in range(2):
            for copy in init_copies(slot):
                copy.start()

    barrier = pltpu.get_barrier_semaphore()

    @pl.loop(0, MATS)
    def _(peer):
        @pl.when(peer != me)
        def _():
            pl.semaphore_signal(barrier, inc=1, device_id=(section, peer), device_id_type=MESH)

    @pl.when(section > 0)
    def _():
        pl.semaphore_signal(barrier, inc=1, device_id=(section - 1, me), device_id_type=MESH)

    @pl.when(section < sections - 1)
    def _():
        pl.semaphore_signal(barrier, inc=1, device_id=(section + 1, me), device_id_type=MESH)

    has_last = (section + sections - 1) // sections
    has_next = (2 * sections - 2 - section) // sections
    pl.semaphore_wait(barrier, MATS - 1 + has_last + has_next)

    lane = lax.broadcasted_iota(jnp.int32, (tall, MAIN), 1)
    low = lane < rest
    row_id = lax.broadcasted_iota(jnp.int32, (rows, win), 0)
    col_id = lax.broadcasted_iota(jnp.int32, (rows, win), 1)
    target = jnp.where(odd == 0, row_id, jnp.where(row_id < MAIN, row_id + win - MAIN, row_id + rest))
    on_diag = col_id == target
    win_cols = pl.ds(pl.multiple_of((me // 2) * win, MAIN), win)

    def transpose_chunk(q):
        cols = pl.ds(pl.multiple_of(q * win, MAIN), win)

        @pl.loop(0, nch // MAIN)
        def _(r):
            part = pl.ds(pl.multiple_of(r * MAIN, MAIN), MAIN)
            vecs_t[cols, part] = vecs[part, cols].T

    def transpose_in_place(block=256):
        @pl.loop(0, nch // block)
        def _(i):
            @pl.loop(i, nch // block)
            def _(j):
                a = pl.ds(pl.multiple_of(i * block, block), block)
                b = pl.ds(pl.multiple_of(j * block, block), block)
                upper = vecs_t[a, b].T
                lower = vecs_t[b, a].T
                vecs_t[b, a] = upper
                vecs_t[a, b] = lower

    def slice_copy():
        return pltpu.make_async_remote_copy(
            src_ref=outer.at[odd], dst_ref=outer.at[0],
            send_sem=slice_send_sem, recv_sem=slice_recv_sem,
            device_id=(section + 1, me), device_id_type=MESH,
        )

    def slice_arrival():
        return pltpu.make_async_remote_copy(
            src_ref=outer.at[0], dst_ref=outer.at[0],
            send_sem=slice_send_sem, recv_sem=slice_recv_sem,
            device_id=(section - 1, me), device_id_type=MESH,
        )

    def stream_rows(q):
        return pl.ds(pl.multiple_of(q * win, MAIN), win)

    def stream_copy(q):
        return pltpu.make_async_remote_copy(
            src_ref=vecs_t.at[stream_rows(q)], dst_ref=vecs.at[stream_rows(q)],
            send_sem=stream_send_sem.at[q], recv_sem=stream_recv_sem.at[q],
            device_id=(section + 1, me), device_id_type=MESH,
        )

    def stream_arrival(q):
        return pltpu.make_async_remote_copy(
            src_ref=vecs.at[stream_rows(q)], dst_ref=vecs.at[stream_rows(q)],
            send_sem=stream_send_sem.at[q], recv_sem=stream_recv_sem.at[q],
            device_id=(section - 1, me), device_id_type=MESH,
        )

    chunks = nch // win

    def prepare_odd():
        for h in range(2):
            load(h, vecs_t).wait()

        @pl.when(section < last)
        def _():
            @pl.loop(0, nch // MAIN)
            def _(r):
                part = pl.ds(pl.multiple_of(r * MAIN, MAIN), MAIN)
                turned = vecs_t[part, win_cols].T
                outer[0, :, part] = turned[:rows]
                outer[1, :, part] = turned[rows:]
            slice_copy().start()
            slice_copy().wait_send()

        @pl.when(section == 1)
        def _():
            for h in range(2):
                load_too(h).wait()

        @pl.when(section > 1)
        def _():
            @pl.loop(0, chunks)
            def _(q):
                stream_arrival(q).wait_recv()
                outer[0] = vecs[pl.ds(pl.multiple_of(q * win, MAIN), rows), :]
                outer[1] = vecs[pl.ds(pl.multiple_of(q * win + rows, rest), rows), :]
                for n in range(SIDE):
                    cols = slice(n * tile, (n + 1) * tile)
                    block = f_dot(outer[...].reshape(win, nch), vecs_t[:, cols])
                    vecs[stream_rows(q), cols] = block.astype(bf16)
        transpose_in_place()

    def near(axis, step):
        if axis == 0:
            return ((y + step + SIDE) % SIDE) * SIDE + z
        return y * SIDE + (z + step + SIDE) % SIDE

    def ring_block(part, group, step):
        first, second = 1 - part, part
        shift = {first: 0, second: 0}
        if group == 0:
            shift[first] = step
        else:
            shift[first] = group - 1
            shift[second] = step
        return ((y + shift[0] + SIDE) % SIDE) * SIDE + (z + shift[1] + SIDE) % SIDE

    def ring_copy(part, group, kind, arriving=False):
        axis = (1 - part) if group == 0 else part
        origin = (0, 0, -1, 1)[kind]
        if arriving:
            origin = (-1, 1, -2, 2)[kind]
        direction = (1, -1, 1, -1)[kind]
        start = ring_block(part, group, origin) * rows + (tall if kind == 3 else 0)
        size = rows if kind < 2 else tall
        region = vecs.at[pl.ds(pl.multiple_of(start, 32), size), pl.ds(part * half, half)]
        return pltpu.make_async_remote_copy(
            src_ref=region, dst_ref=region,
            send_sem=ring_send_sem.at[part, group, kind],
            recv_sem=ring_recv_sem.at[part, group, kind],
            device_id=(section, near(axis, -direction if arriving else direction)),
            device_id_type=MESH,
        )

    def ring_pass(part, group):
        ring_copy(part, group, 0, True).wait_recv()
        ring_copy(part, group, 2).start()
        ring_copy(part, group, 1, True).wait_recv()
        ring_copy(part, group, 3).start()

    def prepare_even():
        for h in range(2):
            load(h, vecs).wait()

        @pl.when(section > 0)
        def _():
            @pl.loop(0, chunks)
            def _(q):
                transpose_chunk(q)
                stream_copy(q).start()

            slice_arrival().wait_recv()
            for n in range(SIDE):
                cols = slice(n * tile, (n + 1) * tile)
                outer[1, :, cols] = f_dot(outer[0], vecs[:, cols]).astype(bf16)
            for axis in range(2):
                for step in (1, -1):
                    pl.semaphore_signal(
                        ready_sem, inc=1, device_id=(section, near(axis, step)), device_id_type=MESH
                    )
            vecs[pl.ds(pl.multiple_of(me * rows, rest), rows), :] = outer[1]
            pl.semaphore_wait(ready_sem, 4)
            for part in range(2):
                for group in range(2):
                    for kind in range(2):
                        ring_copy(part, group, kind).start()
            for part in range(2):
                ring_pass(part, 0)
            for part in range(2):
                for group in (2, 4):
                    for kind in range(2):
                        ring_copy(part, group, kind).start()
            for part in range(2):
                ring_pass(part, 1)
            for part in range(2):
                for kind in (2, 3):
                    ring_copy(part, 0, kind, True).wait_recv()
                for kind in range(2):
                    ring_copy(part, 3, kind).start()
            for group in (2, 4, 3):
                for part in range(2):
                    ring_pass(part, group)
            for group in range(1, 5):
                for part in range(2):
                    for kind in (2, 3):
                        ring_copy(part, group, kind, True).wait_recv()
            for part in range(2):
                for group in range(5):
                    for kind in range(4):
                        ring_copy(part, group, kind).wait_send()

            @pl.loop(0, chunks)
            def _(q):
                stream_copy(q).wait_send()

    def block_copy(trip, slot, place, dest):
        return pltpu.make_async_remote_copy(
            src_ref=send.at[slot, place],
            dst_ref=recv.at[trip, slot, me],
            send_sem=send_sem.at[slot, place],
            recv_sem=recv_sem.at[trip, slot, me],
            device_id=(section, dest),
            device_id_type=MESH,
        )

    def block_arrival(trip, slot, source):
        return pltpu.make_async_remote_copy(
            src_ref=send.at[slot, 0],
            dst_ref=recv.at[trip, slot, source],
            send_sem=send_sem.at[slot, 0],
            recv_sem=recv_sem.at[trip, slot, source],
            device_id=(section, source),
            device_id_type=MESH,
        )

    def ship(trip, slot, step, value):
        main_t = value[:MAIN].astype(bf16).T
        rest_t = value[rest:].T
        for j in range(SIDE):
            base = rows * j
            if j % 2 == 0:
                main = main_t[base:base + rows]
                top = rest_t[base:base + tall]
                bottom = rest_t[base + tall:base + rows]
            else:
                main = jnp.concatenate([main_t[base + rest:base + rows], main_t[base:base + rest]], 0)
                top = rest_t[base + rest:base + rest + tall]
                bottom = jnp.concatenate([rest_t[base + rest + tall:base + rows], rest_t[base:base + rest]], 0)
            packed = jnp.where(low, pltpu.roll(top, rest, 1), bottom)
            place = SIDE * step + j
            send[slot, place, :rows] = main
            send[slot, place, rows:] = packed.astype(bf16)
        for j in range(SIDE):
            place = SIDE * step + j
            dest = y_order[step] * SIDE + j
            if step < SIDE - 1:
                block_copy(trip, slot, place, dest).start()
            else:
                @pl.when(j != z)
                def _():
                    block_copy(trip, slot, place, dest).start()
        if step == SIDE - 1:
            recv[trip, slot, me] = send[slot, SIDE * step + z]

    def tile_cols(step):
        return pl.ds(pl.multiple_of(y_order[step] * tile, MAIN), tile)

    def ship_all(trip, slot, product):
        value = product(0)
        for step in range(SIDE):
            after = product(step + 1) if step < SIDE - 1 else None
            ship(trip, slot, step, value)
            value = after

    def wait_sent(trip, slot):
        for place in range(MATS):
            dest = y_order[place // SIDE] * SIDE + place % SIDE
            if place < MATS - SIDE:
                block_copy(trip, slot, place, dest).wait_send()
            else:
                @pl.when(place % SIDE != z)
                def _():
                    block_copy(trip, slot, place, dest).wait_send()

    def gather_half(trip, slot, which, own):
        for n in range(MATS // 2):
            source = which * (MATS // 2) + n
            if own:
                @pl.when(source != me)
                def _():
                    block_arrival(trip, slot, source).wait_recv()
            else:
                block_arrival(trip, slot, source).wait_recv()
        for q in range(MATS // 4):
            even = which * (MATS // 2) + 2 * q
            base = win * q
            half_lhs[:, base:base + MAIN] = recv[trip, slot, even, :rows]
            half_lhs[:, base + 2 * MAIN:base + 3 * MAIN] = recv[trip, slot, even + 1, :rows]
            left = recv[trip, slot, even, rows:].astype(f32)
            right = recv[trip, slot, even + 1, rows:].astype(f32)
            top = jnp.where(low, left, pltpu.roll(right, rest, 1))
            bottom = jnp.where(low, pltpu.roll(left, rest, 1), right)
            half_lhs[:tall, base + MAIN:base + 2 * MAIN] = top.astype(bf16)
            half_lhs[tall:, base + MAIN:base + 2 * MAIN] = bottom.astype(bf16)

    def dot(a, b):
        return jnp.dot(a, b, preferred_element_type=f32)

    def half_rows(which):
        return pl.ds(pl.multiple_of(which * half, MAIN), half)

    def pass_copy(slot, n, source):
        part = pl.ds(n * tile, tile)
        return pltpu.make_async_remote_copy(
            src_ref=source.at[slot, :, part],
            dst_ref=rmat.at[slot, :, part],
            send_sem=pass_send_sem.at[slot, n],
            recv_sem=pass_recv_sem.at[slot, n],
            device_id=(section + 1, me),
            device_id_type=MESH,
        )

    def pass_arrival(slot, n):
        part = pl.ds(n * tile, tile)
        return pltpu.make_async_remote_copy(
            src_ref=rmat.at[slot, :, part],
            dst_ref=rmat.at[slot, :, part],
            send_sem=pass_send_sem.at[slot, n],
            recv_sem=pass_recv_sem.at[slot, n],
            device_id=(section - 1, me),
            device_id_type=MESH,
        )

    def left_half(slot):
        @pl.when(section == 0)
        def _():
            for copy in init_copies(slot):
                copy.wait()

        for h in range(2):
            @pl.when(section > 0)
            def _():
                for n in range(2 * h, 2 * h + 2):
                    pass_arrival(slot, n).wait_recv()

            if h == 0:
                for n in range(2):
                    cols = slice(n * half, (n + 1) * half)
                    inner[slot, :, cols] = dot(rmat[slot, :, :half], vecs[:half, cols])

        def product(step):
            cols = tile_cols(step)
            return inner[slot, :, cols] + dot(rmat[slot, :, half:], vecs[half:, cols])

        ship_all(0, slot, product)

    def diag_copy(slot, dest):
        return pltpu.make_async_remote_copy(
            src_ref=diag_send.at[slot],
            dst_ref=diag_recv.at[slot, me],
            send_sem=diag_send_sem.at[slot, dest],
            recv_sem=diag_recv_sem.at[slot, me],
            device_id=(section, dest),
            device_id_type=MESH,
        )

    def diag_arrival(slot, source):
        return pltpu.make_async_remote_copy(
            src_ref=diag_send.at[slot],
            dst_ref=diag_recv.at[slot, source],
            send_sem=diag_send_sem.at[slot, source],
            recv_sem=diag_recv_sem.at[slot, source],
            device_id=(section, source),
            device_id_type=MESH,
        )

    def inner_product(slot):
        gather_half(0, slot, far_half, False)
        for n in range(2):
            cols = slice(n * half, (n + 1) * half)
            inner[slot, :, cols] = dot(half_lhs[...], vecs[half_rows(far_half), cols])
        gather_half(0, slot, own_half, True)

        def finish(step):
            cols = tile_cols(step)
            inner[slot, :, cols] += dot(half_lhs[...], vecs[half_rows(own_half), cols])

        finish(SIDE - 1)
        mine = jnp.sum(jnp.where(on_diag, inner[slot, :, win_cols], 0.0), axis=0, keepdims=True)
        diag_send[slot] = jnp.zeros(diag_send.shape[1:], f32)
        for n in range(win // MAIN):
            diag_send[slot, n:n + 1, :] = mine[:, n * MAIN:(n + 1) * MAIN]
        diag_recv[slot, me] = diag_send[slot]

        @pl.loop(0, MATS)
        def _(dest):
            @pl.when(dest != me)
            def _():
                diag_copy(slot, dest).start()

        for step in range(SIDE - 1):
            finish(step)

    def propagate(slot):
        @pl.loop(0, MATS)
        def _(source):
            @pl.when(source != me)
            def _():
                diag_arrival(slot, source).wait_recv()

        pieces = []
        for p in range(MATS // 2):
            pair = diag_recv[slot, 2 * p] + diag_recv[slot, 2 * p + 1]
            pieces += [pair[n:n + 1, :] for n in range(win // MAIN)]
        full_diag = jnp.concatenate(pieces, axis=1)
        g_one = g_one_ref[pl.ds(slot, 1), :]
        g_two = g_two_ref[pl.ds(slot, 1), :]
        precond = 1.0 / (g_one + jnp.abs(full_diag))
        side = g_two * precond
        term = g_one - 2.0 * g_two * g_two * precond + g_one * side * side
        side_ref[0:1, :] = side
        side_ref[1:2, :] = term
        side_win = side_ref[0:1, win_cols]
        term_win = side_ref[1:2, win_cols]
        side_rows = jnp.sum(jnp.where(on_diag, side_win, 0.0), axis=1, keepdims=True)
        scaled = side_rows * inner[slot, :, win_cols] * side_win
        outer[slot, :, win_cols] = (scaled + jnp.where(on_diag, term_win, 0.0)).astype(bf16)
        for q in range(nch // win):
            cols = slice(q * win, (q + 1) * win)

            @pl.when(q != me // 2)
            def _():
                outer[slot, :, cols] = (side_rows * inner[slot, :, cols] * side[:, cols]).astype(bf16)

            if q % 2 == 1:
                @pl.when((section > 0) & (section < last))
                def _():
                    pass_copy(slot, q // 2, outer).start()

        @pl.when((section % 2 == 1) & (section > 1) & (section < last) & (slot == 1))
        def _():
            pl.semaphore_signal(go_sem, inc=1, device_id=(section - 1, me), device_id_type=MESH)

    def flip_out(slot):
        @pl.when((slot == 0) & (section < last - 1))
        def _():
            pl.semaphore_wait(go_sem, 1)

        for n in range(SIDE):
            pass_copy(slot, n, outer).wait_send()
        wait_sent(0, slot)
        ship_all(2, slot, lambda step: outer[slot, :, tile_cols(step)].astype(f32))

    def flip_in(slot):
        for which, own in ((far_half, False), (own_half, True)):
            gather_half(2, slot, which, own)
            outer[slot, :, half_rows(which)] = half_lhs[...]

    def right_half(slot):
        wait_sent(1, slot)
        ship_all(1, slot, lambda step: dot(outer[slot], vecs_t[:, tile_cols(step)]))

    def next_rows(slot):
        gather_half(1, slot, far_half, False)
        for n in range(2):
            cols = slice(n * half, (n + 1) * half)
            inner[slot, :, cols] = dot(half_lhs[...], vecs_t[half_rows(far_half), cols])
        gather_half(1, slot, own_half, True)
        for n in range(SIDE):
            cols = slice(n * tile, (n + 1) * tile)
            value = inner[slot, :, cols] + dot(half_lhs[...], vecs_t[half_rows(own_half), cols])
            rmat[slot, :, cols] = value.astype(bf16)

            @pl.when(section == 0)
            def _():
                pass_copy(slot, n, rmat).start()
        for copy in out_copies(slot):
            copy.start()

    @pl.when(even_section)
    def _():
        prepare_even()

    @pl.when(section % 2 == 1)
    def _():
        prepare_odd()

    def turn(part):
        @pl.loop(part * (chunks // 2), (part + 1) * (chunks // 2))
        def _(q):
            transpose_chunk(q)

    stages = [left_half, inner_product, propagate, right_half, next_rows, flip_out, flip_in, turn]
    is_first = 1 - (section + last) // sections
    is_last = section // last
    is_flipped = (1 - section % 2) * (1 - is_first)
    is_plain = 1 - is_first - is_last - is_flipped
    now, later = (
        is_first * a + is_last * b + is_flipped * c + is_plain * d
        for a, b, c, d in zip(*(digits(order) for order in (FIRST, LAST, FLIPPED, PLAIN)))
    )

    def step(_, queue):
        now, later = queue
        code = now % BASE
        stage, slot = code // 2, code % 2
        for n, run in enumerate(stages):
            @pl.when(stage == n)
            def _():
                run(slot)
        return now // BASE + (later % BASE) * BASE ** (DIGITS - 1), later // BASE

    lax.fori_loop(0, STEPS, step, (now, later))

    @pl.loop(0, 2)
    def _(slot):
        wait_sent(1, slot)
        for copy in out_copies(slot):
            copy.wait()

        @pl.loop(0, MATS)
        def _(dest):
            @pl.when(dest != me)
            def _():
                diag_copy(slot, dest).wait_send()

        @pl.when((section < last) & jnp.logical_not(flipped))
        def _():
            for n in range(SIDE):
                pass_copy(slot, n, rmat).wait_send()


def on_device(sections, eigvec, eig_level, energies, order, init_r):
    nch = eigvec.shape[1]
    rows = init_r.shape[1]
    g_one, g_two = greens(eig_level[0][None, :], jnp.take(energies, order)[:, None])
    initial = jnp.take(init_r, order, axis=0)
    any_spec = pl.BlockSpec(memory_space=pl.ANY)
    vmem_spec = pl.BlockSpec(memory_space=pltpu.VMEM)
    dma = pltpu.SemaphoreType.DMA
    bf16, f32 = jnp.bfloat16, jnp.float32
    block = rows + rows // 2
    return pl.pallas_call(
        functools.partial(kernel, sections),
        out_shape=jax.ShapeDtypeStruct((1, 2, rows, nch), bf16),
        in_specs=[any_spec, vmem_spec, vmem_spec, any_spec],
        out_specs=any_spec,
        scratch_shapes=[
            pltpu.VMEM((nch, nch), bf16),
            pltpu.VMEM((nch, nch), bf16),
            pltpu.VMEM((2, rows, nch), bf16),
            pltpu.VMEM((2, rows, nch), f32),
            pltpu.VMEM((2, rows, nch), bf16),
            pltpu.VMEM((rows, nch // 2), bf16),
            pltpu.VMEM((2, MATS, block, MAIN), bf16),
            pltpu.VMEM((3, 2, MATS, block, MAIN), bf16),
            pltpu.VMEM((2, 8, MAIN), f32),
            pltpu.VMEM((2, MATS, 8, MAIN), f32),
            pltpu.VMEM((2, nch), f32),
            dma((4,)),
            dma((2, 2)),
            dma((2, 2)),
            dma((2, MATS)),
            dma((3, 2, MATS)),
            dma((2, MATS)),
            dma((2, MATS)),
            dma((2, SIDE)),
            dma((2, SIDE)),
            dma(()),
            dma(()),
            dma((nch // (2 * rows),)),
            dma((nch // (2 * rows),)),
            dma((2, 5, SIDE)),
            dma((2, 5, SIDE)),
            pltpu.SemaphoreType.REGULAR,
            pltpu.SemaphoreType.REGULAR,
        ],
        compiler_params=pltpu.CompilerParams(
            collective_id=0, has_side_effects=True, vmem_limit_bytes=67043328
        ),
        name="sectors",
    )(eigvec, g_one, g_two, initial)


def solution(mesh):
    in_specs = (P("section", None, None), P("section", None), P(), P(), P(None, "mat", None))
    out_specs = P("section", None, "mat", None)
    return jax.shard_map(
        functools.partial(on_device, mesh.shape["section"]),
        mesh=mesh, in_specs=in_specs, out_specs=out_specs, check_vma=False,
    )
```

```python
import functools

import jax
import jax.numpy as jnp
from jax import lax
from jax.experimental import pallas as pl
from jax.experimental.pallas import tpu as pltpu
from jax.sharding import PartitionSpec as P

MESH = pl.DeviceIdType.MESH
SIDE = 4
MATS = SIDE * SIDE
MAIN = 128
sector_width = 1.0


LEFT, INNER, PROPAGATE, RIGHT, NEXT, FLIP_OUT, FLIP_IN, TURN = range(8)
FIRST = [
    (LEFT, 0), (TURN, 0), (INNER, 0), (TURN, 1), (PROPAGATE, 0), (RIGHT, 0), (LEFT, 1),
    (NEXT, 0), (INNER, 1), (PROPAGATE, 1), (RIGHT, 1), (NEXT, 1),
]
CHAIN = [
    (LEFT, 0), (INNER, 0), (PROPAGATE, 0), (LEFT, 1), (INNER, 1), (PROPAGATE, 1),
]
PLAIN = CHAIN + [(TURN, 0), (RIGHT, 0), (RIGHT, 1), (NEXT, 0), (NEXT, 1)]
FLIPPED = CHAIN + [
    (FLIP_OUT, 0), (FLIP_OUT, 1), (FLIP_IN, 0), (RIGHT, 0), (FLIP_IN, 1), (RIGHT, 1),
    (NEXT, 0), (NEXT, 1),
]
LAST = [
    (LEFT, 0), (INNER, 0), (PROPAGATE, 0), (LEFT, 1), (RIGHT, 0), (INNER, 1), (NEXT, 0),
    (PROPAGATE, 1), (RIGHT, 1), (NEXT, 1),
]
STEPS, BASE, DIGITS = 14, 17, 7


def digits(order):
    codes = [2 * stage + slot for stage, slot in order]
    codes += [BASE - 1] * (STEPS - len(codes))
    return [
        sum(code * BASE ** n for n, code in enumerate(codes[part:part + DIGITS]))
        for part in (0, DIGITS)
    ]


def greens(levels, energy):
    wave_number = jnp.sqrt(levels - energy)
    phase_arg = wave_number * sector_width
    sinh_value = jnp.sinh(phase_arg)
    g_one = jnp.cosh(phase_arg) / (wave_number * sinh_value)
    g_two = 1.0 / (wave_number * sinh_value)
    return (g_one, g_two)


def kernel(
    sections,
    eig_ref, g_one_ref, g_two_ref, init_ref, order_ref, out_ref,
    vecs, vecs_t, rmat, inner, outer, half_lhs, send, recv, diag_send, diag_recv, side_ref,
    load_sem, init_sem, out_sem, send_sem, recv_sem, diag_send_sem, diag_recv_sem,
    pass_send_sem, pass_recv_sem, slice_send_sem, slice_recv_sem, stream_send_sem, stream_recv_sem,
    ring_send_sem, ring_recv_sem, ready_sem, go_sem, clear_sem,
):
    nch = vecs.shape[0]
    rows = rmat.shape[1]
    rest = rows - MAIN
    tall = rows // 2
    half = nch // 2
    tile = rows * SIDE
    win = 2 * rows
    f32, bf16 = jnp.float32, jnp.bfloat16

    section = lax.axis_index("section")
    me = lax.axis_index("mat")
    y, z = me // SIDE, me % SIDE
    odd = me % 2
    y_order = [(y + 2) % SIDE, SIDE - 1 - y, y + 1 - 2 * (y % 2), y]
    even_section = section % 2 == 0
    flipped = even_section & (section >= 2)
    last = sections - 1
    late_turn = 3
    f_dot = functools.partial(jnp.dot, preferred_element_type=f32)

    def load(h, space):
        part = pl.ds(h * half, half)
        return pltpu.make_async_copy(eig_ref.at[0, part], space.at[part], load_sem.at[h])

    def load_too(h):
        part = pl.ds(h * half, half)
        return pltpu.make_async_copy(eig_ref.at[0, part], vecs.at[part], load_sem.at[2 + h])

    @pl.when(even_section)
    def _():
        for h in range(2):
            load(h, vecs).start()

    @pl.when(section % 2 == 1)
    def _():
        for h in range(2):
            load(h, vecs_t).start()

    @pl.when(section == 1)
    def _():
        for h in range(2):
            load_too(h).start()

    def row_copies(slot):
        first = pl.multiple_of(odd * rest, rest)
        second = pl.multiple_of(MAIN * (1 - odd), rest)
        return ((pl.ds(first, MAIN), pl.ds(0, MAIN)), (pl.ds(second, rest), pl.ds(MAIN, rest)))

    def init_copies(slot):
        return [
            pltpu.make_async_copy(init_ref.at[slot, a], outer.at[slot, b], init_sem.at[slot, n])
            for n, (a, b) in enumerate(row_copies(slot))
        ]

    def out_copies(slot):
        return [
            pltpu.make_async_copy(rmat.at[slot, b], out_ref.at[0, slot, a], out_sem.at[slot, n])
            for n, (a, b) in enumerate(row_copies(slot))
        ]

    @pl.when(section == 0)
    def _():
        for slot in range(2):
            for copy in init_copies(slot):
                copy.start()

    barrier = pltpu.get_barrier_semaphore()

    @pl.loop(0, MATS)
    def _(peer):
        @pl.when(peer != me)
        def _():
            pl.semaphore_signal(barrier, inc=1, device_id=(section, peer), device_id_type=MESH)

    @pl.when(section > 0)
    def _():
        pl.semaphore_signal(barrier, inc=1, device_id=(section - 1, me), device_id_type=MESH)

    @pl.when(section < sections - 1)
    def _():
        pl.semaphore_signal(barrier, inc=1, device_id=(section + 1, me), device_id_type=MESH)

    has_last = (section + sections - 1) // sections
    has_next = (2 * sections - 2 - section) // sections
    pl.semaphore_wait(barrier, MATS - 1 + has_last + has_next)

    lane = lax.broadcasted_iota(jnp.int32, (tall, MAIN), 1)
    low = lane < rest
    row_id = lax.broadcasted_iota(jnp.int32, (rows, win), 0)
    col_id = lax.broadcasted_iota(jnp.int32, (rows, win), 1)
    target = jnp.where(odd == 0, row_id, jnp.where(row_id < MAIN, row_id + win - MAIN, row_id + rest))
    on_diag = col_id == target
    win_cols = pl.ds(pl.multiple_of((me // 2) * win, MAIN), win)

    def transpose_rows(first, count):
        @pl.loop(first, first + count)
        def _(r):
            part = pl.ds(pl.multiple_of(r * MAIN, MAIN), MAIN)
            vecs_t[:, part] = vecs[part, :].T

    def transpose_in_place(block=256):
        @pl.loop(0, nch // block)
        def _(i):
            @pl.loop(i, nch // block)
            def _(j):
                a = pl.ds(pl.multiple_of(i * block, block), block)
                b = pl.ds(pl.multiple_of(j * block, block), block)
                upper = vecs_t[a, b].T
                lower = vecs_t[b, a].T
                vecs_t[b, a] = upper
                vecs_t[a, b] = lower

    def slice_copy():
        return pltpu.make_async_remote_copy(
            src_ref=outer.at[odd], dst_ref=outer.at[0],
            send_sem=slice_send_sem, recv_sem=slice_recv_sem,
            device_id=(section + 1, me), device_id_type=MESH,
        )

    def slice_arrival():
        return pltpu.make_async_remote_copy(
            src_ref=outer.at[0], dst_ref=outer.at[0],
            send_sem=slice_send_sem, recv_sem=slice_recv_sem,
            device_id=(section - 1, me), device_id_type=MESH,
        )

    def stream_rows(q):
        return pl.ds(pl.multiple_of(q * win, MAIN), win)

    def stream_copy(q):
        return pltpu.make_async_remote_copy(
            src_ref=vecs_t.at[stream_rows(q)], dst_ref=vecs.at[stream_rows(q)],
            send_sem=stream_send_sem.at[q], recv_sem=stream_recv_sem.at[q],
            device_id=(section + 1, me), device_id_type=MESH,
        )

    def stream_arrival(q):
        return pltpu.make_async_remote_copy(
            src_ref=vecs.at[stream_rows(q)], dst_ref=vecs.at[stream_rows(q)],
            send_sem=stream_send_sem.at[q], recv_sem=stream_recv_sem.at[q],
            device_id=(section - 1, me), device_id_type=MESH,
        )

    chunks = nch // win

    def prepare_odd():
        for h in range(2):
            load(h, vecs_t).wait()

        @pl.when(section < last)
        def _():
            @pl.loop(0, nch // MAIN)
            def _(r):
                part = pl.ds(pl.multiple_of(r * MAIN, MAIN), MAIN)
                turned = vecs_t[part, win_cols].T
                outer[0, :, part] = turned[:rows]
                outer[1, :, part] = turned[rows:]
            slice_copy().start()
            slice_copy().wait_send()

        @pl.when(section == 1)
        def _():
            for h in range(2):
                load_too(h).wait()

        @pl.when(section > 1)
        def _():
            @pl.loop(0, chunks)
            def _(q):
                stream_arrival(q).wait_recv()
                outer[0] = vecs[pl.ds(pl.multiple_of(q * win, MAIN), rows), :]
                outer[1] = vecs[pl.ds(pl.multiple_of(q * win + rows, rest), rows), :]
                for n in range(SIDE):
                    cols = slice(n * tile, (n + 1) * tile)
                    block = f_dot(outer[...].reshape(win, nch), vecs_t[:, cols])
                    vecs[stream_rows(q), cols] = block.astype(bf16)

        @pl.when(section != late_turn)
        def _():
            transpose_in_place()

    def near(axis, step):
        if axis == 0:
            return ((y + step + SIDE) % SIDE) * SIDE + z
        return y * SIDE + (z + step + SIDE) % SIDE

    def ring_block(part, group, step):
        first, second = 1 - part, part
        shift = {first: 0, second: 0}
        if group == 0:
            shift[first] = step
        else:
            shift[first] = group - 1
            shift[second] = step
        return ((y + shift[0] + SIDE) % SIDE) * SIDE + (z + shift[1] + SIDE) % SIDE

    def ring_copy(part, group, kind, arriving=False):
        axis = (1 - part) if group == 0 else part
        origin = (0, 0, -1, 1)[kind]
        if arriving:
            origin = (-1, 1, -2, 2)[kind]
        direction = (1, -1, 1, -1)[kind]
        start = ring_block(part, group, origin) * rows + (tall if kind == 3 else 0)
        size = rows if kind < 2 else tall
        region = vecs.at[pl.ds(pl.multiple_of(start, 32), size), pl.ds(part * half, half)]
        return pltpu.make_async_remote_copy(
            src_ref=region, dst_ref=region,
            send_sem=ring_send_sem.at[part, group, kind],
            recv_sem=ring_recv_sem.at[part, group, kind],
            device_id=(section, near(axis, -direction if arriving else direction)),
            device_id_type=MESH,
        )

    def ring_pass(part, group):
        ring_copy(part, group, 0, True).wait_recv()
        ring_copy(part, group, 2).start()
        ring_copy(part, group, 1, True).wait_recv()
        ring_copy(part, group, 3).start()

    def prepare_even():
        @pl.when(section == 0)
        def _():
            for slot in range(2):
                for copy in init_copies(slot):
                    copy.wait()
            for slot in range(2):
                rmat[slot] = jnp.where(order_ref[slot] == 0, outer[0], outer[1])

        for h in range(2):
            load(h, vecs).wait()

        @pl.when(section > 0)
        def _():
            transpose_rows(0, nch // MAIN)

            @pl.loop(0, chunks)
            def _(q):
                stream_copy(q).start()

            slice_arrival().wait_recv()
            for n in range(SIDE):
                cols = slice(n * tile, (n + 1) * tile)
                outer[1, :, cols] = f_dot(outer[0], vecs[:, cols]).astype(bf16)
            for axis in range(2):
                for step in (1, -1):
                    pl.semaphore_signal(
                        ready_sem, inc=1, device_id=(section, near(axis, step)), device_id_type=MESH
                    )
            vecs[pl.ds(pl.multiple_of(me * rows, rest), rows), :] = outer[1]
            pl.semaphore_wait(ready_sem, 4)
            for part in range(2):
                for group in range(2):
                    for kind in range(2):
                        ring_copy(part, group, kind).start()
            for part in range(2):
                ring_pass(part, 0)
            for part in range(2):
                for group in (2, 4):
                    for kind in range(2):
                        ring_copy(part, group, kind).start()
            for part in range(2):
                ring_pass(part, 1)
            for part in range(2):
                for kind in (2, 3):
                    ring_copy(part, 0, kind, True).wait_recv()
                for kind in range(2):
                    ring_copy(part, 3, kind).start()
            for group in (2, 4, 3):
                for part in range(2):
                    ring_pass(part, group)
            for group in range(1, 5):
                for part in range(2):
                    for kind in (2, 3):
                        ring_copy(part, group, kind, True).wait_recv()
            for part in range(2):
                for group in range(5):
                    for kind in range(4):
                        ring_copy(part, group, kind).wait_send()

            @pl.loop(0, chunks)
            def _(q):
                stream_copy(q).wait_send()

    def block_copy(trip, slot, place, dest):
        return pltpu.make_async_remote_copy(
            src_ref=send.at[slot, place],
            dst_ref=recv.at[trip, slot, me],
            send_sem=send_sem.at[slot, place],
            recv_sem=recv_sem.at[trip, slot, me],
            device_id=(section, dest),
            device_id_type=MESH,
        )

    def block_arrival(trip, slot, source):
        return pltpu.make_async_remote_copy(
            src_ref=send.at[slot, 0],
            dst_ref=recv.at[trip, slot, source],
            send_sem=send_sem.at[slot, 0],
            recv_sem=recv_sem.at[trip, slot, source],
            device_id=(section, source),
            device_id_type=MESH,
        )

    def ship(trip, slot, step, value):
        main_t = value[:MAIN].astype(bf16).T
        rest_t = value[rest:].T
        for j in range(SIDE):
            base = rows * j
            if j % 2 == 0:
                main = main_t[base:base + rows]
                top = rest_t[base:base + tall]
                bottom = rest_t[base + tall:base + rows]
            else:
                main = jnp.concatenate([main_t[base + rest:base + rows], main_t[base:base + rest]], 0)
                top = rest_t[base + rest:base + rest + tall]
                bottom = jnp.concatenate([rest_t[base + rest + tall:base + rows], rest_t[base:base + rest]], 0)
            packed = jnp.where(low, pltpu.roll(top, rest, 1), bottom)
            place = SIDE * step + j
            send[slot, place, :rows] = main
            send[slot, place, rows:] = packed.astype(bf16)
        for j in range(SIDE):
            place = SIDE * step + j
            dest = y_order[step] * SIDE + j
            if step < SIDE - 1:
                block_copy(trip, slot, place, dest).start()
            else:
                @pl.when(j != z)
                def _():
                    block_copy(trip, slot, place, dest).start()
        if step == SIDE - 1:
            recv[trip, slot, me] = send[slot, SIDE * step + z]

    def tile_cols(step):
        return pl.ds(pl.multiple_of(y_order[step] * tile, MAIN), tile)

    def ship_all(trip, slot, product):
        value = product(0)
        for step in range(SIDE):
            after = product(step + 1) if step < SIDE - 1 else None
            ship(trip, slot, step, value)
            value = after

    def wait_sent(trip, slot):
        for place in range(MATS):
            dest = y_order[place // SIDE] * SIDE + place % SIDE
            if place < MATS - SIDE:
                block_copy(trip, slot, place, dest).wait_send()
            else:
                @pl.when(place % SIDE != z)
                def _():
                    block_copy(trip, slot, place, dest).wait_send()

    def gather_group(trip, slot, group, own):
        for n in range(SIDE):
            source = group * SIDE + n
            if own:
                @pl.when(source != me)
                def _():
                    block_arrival(trip, slot, source).wait_recv()
            else:
                block_arrival(trip, slot, source).wait_recv()
        for q in range(SIDE // 2):
            even = group * SIDE + 2 * q
            at = pl.multiple_of(group * tile + win * q, MAIN)
            half_lhs[:, pl.ds(at, MAIN)] = recv[trip, slot, even, :rows]
            half_lhs[:, pl.ds(at + 2 * MAIN, MAIN)] = recv[trip, slot, even + 1, :rows]
            left = recv[trip, slot, even, rows:].astype(f32)
            right = recv[trip, slot, even + 1, rows:].astype(f32)
            top = jnp.where(low, left, pltpu.roll(right, rest, 1))
            bottom = jnp.where(low, pltpu.roll(left, rest, 1), right)
            half_lhs[:tall, pl.ds(at + MAIN, MAIN)] = top.astype(bf16)
            half_lhs[tall:, pl.ds(at + MAIN, MAIN)] = bottom.astype(bf16)

    def gather(trip, slot):
        for step in range(SIDE):
            gather_group(trip, slot, y_order[step], step == SIDE - 1)

    def dot(a, b):
        return jnp.dot(a, b, preferred_element_type=f32)

    def pass_copy(slot, n, source):
        part = pl.ds(n * tile, tile)
        return pltpu.make_async_remote_copy(
            src_ref=source.at[slot, :, part],
            dst_ref=rmat.at[slot, :, part],
            send_sem=pass_send_sem.at[slot, n],
            recv_sem=pass_recv_sem.at[slot, n],
            device_id=(section + 1, me),
            device_id_type=MESH,
        )

    def pass_arrival(slot, n):
        part = pl.ds(n * tile, tile)
        return pltpu.make_async_remote_copy(
            src_ref=rmat.at[slot, :, part],
            dst_ref=rmat.at[slot, :, part],
            send_sem=pass_send_sem.at[slot, n],
            recv_sem=pass_recv_sem.at[slot, n],
            device_id=(section - 1, me),
            device_id_type=MESH,
        )

    def left_half(slot):
        @pl.when(flipped & (slot == 1))
        def _():
            pl.semaphore_wait(clear_sem, 1)

        @pl.when(section > 0)
        def _():
            for n in range(SIDE):
                pass_arrival(slot, n).wait_recv()

        def product(step):
            return dot(rmat[slot], vecs[:, tile_cols(step)])

        ship_all(0, slot, product)

    def diag_copy(slot, dest):
        return pltpu.make_async_remote_copy(
            src_ref=diag_send.at[slot],
            dst_ref=diag_recv.at[slot, me],
            send_sem=diag_send_sem.at[slot, dest],
            recv_sem=diag_recv_sem.at[slot, me],
            device_id=(section, dest),
            device_id_type=MESH,
        )

    def diag_arrival(slot, source):
        return pltpu.make_async_remote_copy(
            src_ref=diag_send.at[slot],
            dst_ref=diag_recv.at[slot, source],
            send_sem=diag_send_sem.at[slot, source],
            recv_sem=diag_recv_sem.at[slot, source],
            device_id=(section, source),
            device_id_type=MESH,
        )

    def inner_product(slot):
        gather(0, slot)

        @pl.when((section % 2 == 1) & (section > 1) & (slot == 0))
        def _():
            pl.semaphore_signal(clear_sem, inc=1, device_id=(section - 1, me), device_id_type=MESH)

        def finish(step):
            cols = tile_cols(step)
            inner[slot, :, cols] = dot(half_lhs[...], vecs[:, cols])

        finish(SIDE - 1)
        mine = jnp.sum(jnp.where(on_diag, inner[slot, :, win_cols], 0.0), axis=0, keepdims=True)
        diag_send[slot] = jnp.zeros(diag_send.shape[1:], f32)
        for n in range(win // MAIN):
            diag_send[slot, n:n + 1, :] = mine[:, n * MAIN:(n + 1) * MAIN]
        diag_recv[slot, me] = diag_send[slot]

        @pl.loop(0, MATS)
        def _(dest):
            @pl.when(dest != me)
            def _():
                diag_copy(slot, dest).start()

        for step in range(SIDE - 1):
            finish(step)

    def propagate(slot):
        @pl.loop(0, MATS)
        def _(source):
            @pl.when(source != me)
            def _():
                diag_arrival(slot, source).wait_recv()

        pieces = []
        for p in range(MATS // 2):
            pair = diag_recv[slot, 2 * p] + diag_recv[slot, 2 * p + 1]
            pieces += [pair[n:n + 1, :] for n in range(win // MAIN)]
        full_diag = jnp.concatenate(pieces, axis=1)
        g_one = g_one_ref[pl.ds(slot, 1), :]
        g_two = g_two_ref[pl.ds(slot, 1), :]
        precond = 1.0 / (g_one + jnp.abs(full_diag))
        side = g_two * precond
        term = g_one - 2.0 * g_two * g_two * precond + g_one * side * side
        side_ref[0:1, :] = side
        side_ref[1:2, :] = term
        side_win = side_ref[0:1, win_cols]
        term_win = side_ref[1:2, win_cols]
        side_rows = jnp.sum(jnp.where(on_diag, side_win, 0.0), axis=1, keepdims=True)
        scaled = side_rows * inner[slot, :, win_cols] * side_win
        outer[slot, :, win_cols] = (scaled + jnp.where(on_diag, term_win, 0.0)).astype(bf16)
        for q in range(nch // win):
            cols = slice(q * win, (q + 1) * win)

            @pl.when(q != me // 2)
            def _():
                outer[slot, :, cols] = (side_rows * inner[slot, :, cols] * side[:, cols]).astype(bf16)

            if q % 2 == 1:
                @pl.when((section > 0) & (section < last))
                def _():
                    pass_copy(slot, q // 2, outer).start()

        @pl.when((section % 2 == 1) & (section > 1) & (section < last) & (slot == 1))
        def _():
            pl.semaphore_signal(go_sem, inc=1, device_id=(section - 1, me), device_id_type=MESH)

    def flip_out(slot):
        @pl.when((slot == 0) & (section < last - 1))
        def _():
            pl.semaphore_wait(go_sem, 1)

        for n in range(SIDE):
            pass_copy(slot, n, outer).wait_send()
        wait_sent(0, slot)
        ship_all(2, slot, lambda step: outer[slot, :, tile_cols(step)].astype(f32))

    def flip_in(slot):
        gather(2, slot)
        outer[slot] = half_lhs[...]

    def right_half(slot):
        wait_sent(1, slot)
        ship_all(1, slot, lambda step: dot(outer[slot], vecs_t[:, tile_cols(step)]))

    def next_rows(slot):
        gather(1, slot)
        for n in range(SIDE):
            cols = slice(n * tile, (n + 1) * tile)
            value = dot(half_lhs[...], vecs_t[:, cols])
            rmat[slot, :, cols] = value.astype(bf16)

            @pl.when(section == 0)
            def _():
                pass_copy(slot, n, rmat).start()
        for copy in out_copies(slot):
            copy.start()

    @pl.when(even_section)
    def _():
        prepare_even()

    @pl.when(section % 2 == 1)
    def _():
        prepare_odd()

    def turn(part):
        @pl.when(section == 0)
        def _():
            transpose_rows(part * (nch // MAIN // 2), nch // MAIN // 2)

        @pl.when(section == late_turn)
        def _():
            transpose_in_place()

    stages = [left_half, inner_product, propagate, right_half, next_rows, flip_out, flip_in, turn]
    is_first = 1 - (section + last) // sections
    is_last = section // last
    is_flipped = (1 - section % 2) * (1 - is_first)
    is_plain = 1 - is_first - is_last - is_flipped
    now, later = (
        is_first * a + is_last * b + is_flipped * c + is_plain * d
        for a, b, c, d in zip(*(digits(order) for order in (FIRST, LAST, FLIPPED, PLAIN)))
    )

    def step(_, queue):
        now, later = queue
        code = now % BASE
        stage, slot = code // 2, code % 2
        for n, run in enumerate(stages):
            @pl.when(stage == n)
            def _():
                run(slot)
        return now // BASE + (later % BASE) * BASE ** (DIGITS - 1), later // BASE

    lax.fori_loop(0, STEPS, step, (now, later))

    @pl.loop(0, 2)
    def _(slot):
        wait_sent(1, slot)
        for copy in out_copies(slot):
            copy.wait()

        @pl.loop(0, MATS)
        def _(dest):
            @pl.when(dest != me)
            def _():
                diag_copy(slot, dest).wait_send()

        @pl.when((section < last) & jnp.logical_not(flipped))
        def _():
            for n in range(SIDE):
                pass_copy(slot, n, rmat).wait_send()


def on_device(sections, eigvec, eig_level, energies, order, init_r):
    nch = eigvec.shape[1]
    rows = init_r.shape[1]
    taken = jnp.where(order == 0, energies[0], energies[1])
    g_one, g_two = greens(eig_level[0][None, :], taken[:, None])
    any_spec = pl.BlockSpec(memory_space=pl.ANY)
    vmem_spec = pl.BlockSpec(memory_space=pltpu.VMEM)
    dma = pltpu.SemaphoreType.DMA
    bf16, f32 = jnp.bfloat16, jnp.float32
    block = rows + rows // 2
    return pl.pallas_call(
        functools.partial(kernel, sections),
        out_shape=jax.ShapeDtypeStruct((1, 2, rows, nch), bf16),
        in_specs=[any_spec, vmem_spec, vmem_spec, any_spec, pl.BlockSpec(memory_space=pltpu.SMEM)],
        out_specs=any_spec,
        scratch_shapes=[
            pltpu.VMEM((nch, nch), bf16),
            pltpu.VMEM((nch, nch), bf16),
            pltpu.VMEM((2, rows, nch), bf16),
            pltpu.VMEM((2, rows, nch), f32),
            pltpu.VMEM((2, rows, nch), bf16),
            pltpu.VMEM((rows, nch), bf16),
            pltpu.VMEM((2, MATS, block, MAIN), bf16),
            pltpu.VMEM((3, 2, MATS, block, MAIN), bf16),
            pltpu.VMEM((2, 8, MAIN), f32),
            pltpu.VMEM((2, MATS, 8, MAIN), f32),
            pltpu.VMEM((2, nch), f32),
            dma((4,)),
            dma((2, 2)),
            dma((2, 2)),
            dma((2, MATS)),
            dma((3, 2, MATS)),
            dma((2, MATS)),
            dma((2, MATS)),
            dma((2, SIDE)),
            dma((2, SIDE)),
            dma(()),
            dma(()),
            dma((nch // (2 * rows),)),
            dma((nch // (2 * rows),)),
            dma((2, 5, SIDE)),
            dma((2, 5, SIDE)),
            pltpu.SemaphoreType.REGULAR,
            pltpu.SemaphoreType.REGULAR,
            pltpu.SemaphoreType.REGULAR,
        ],
        compiler_params=pltpu.CompilerParams(
            collective_id=0, has_side_effects=True, vmem_limit_bytes=67043328
        ),
        name="sectors",
    )(eigvec, g_one, g_two, init_r, order)


def solution(mesh):
    in_specs = (P("section", None, None), P("section", None), P(), P(), P(None, "mat", None))
    out_specs = P("section", None, "mat", None)
    return jax.shard_map(
        functools.partial(on_device, mesh.shape["section"]),
        mesh=mesh, in_specs=in_specs, out_specs=out_specs, check_vma=False,
    )
```

```python
import functools

import jax
import jax.numpy as jnp
from jax import lax
from jax.experimental import pallas as pl
from jax.experimental.pallas import tpu as pltpu
from jax.sharding import PartitionSpec as P

MESH = pl.DeviceIdType.MESH
SIDE = 4
MATS = SIDE * SIDE
MAIN = 128
sector_width = 1.0


LEFT, INNER, PROPAGATE, RIGHT, NEXT, FLIP_OUT, FLIP_IN, TURN = range(8)
FIRST = [
    (LEFT, 0), (TURN, 0), (INNER, 0), (TURN, 1), (PROPAGATE, 0), (RIGHT, 0), (LEFT, 1),
    (NEXT, 0), (INNER, 1), (PROPAGATE, 1), (RIGHT, 1), (NEXT, 1),
]
CHAIN = [
    (LEFT, 0), (INNER, 0), (PROPAGATE, 0), (LEFT, 1), (INNER, 1), (PROPAGATE, 1),
]
PLAIN = CHAIN + [(RIGHT, 0), (RIGHT, 1), (NEXT, 0), (NEXT, 1)]
FLIPPED = CHAIN + [
    (FLIP_OUT, 0), (FLIP_OUT, 1), (FLIP_IN, 0), (RIGHT, 0), (FLIP_IN, 1), (RIGHT, 1),
    (NEXT, 0), (NEXT, 1),
]
LAST = [
    (LEFT, 0), (INNER, 0), (PROPAGATE, 0), (LEFT, 1), (RIGHT, 0), (INNER, 1), (PROPAGATE, 1),
    (RIGHT, 1), (NEXT, 0), (NEXT, 1),
]
STEPS, BASE, DIGITS = 14, 17, 7


def digits(order):
    codes = [2 * stage + slot for stage, slot in order]
    codes += [BASE - 1] * (STEPS - len(codes))
    return [
        sum(code * BASE ** n for n, code in enumerate(codes[part:part + DIGITS]))
        for part in (0, DIGITS)
    ]


def greens(levels, energy):
    wave_number = jnp.sqrt(levels - energy)
    phase_arg = wave_number * sector_width
    sinh_value = jnp.sinh(phase_arg)
    g_one = jnp.cosh(phase_arg) / (wave_number * sinh_value)
    g_two = 1.0 / (wave_number * sinh_value)
    return (g_one, g_two)


def kernel(
    sections,
    eig_ref, g_one_ref, g_two_ref, init_ref, order_ref, out_ref,
    vecs, vecs_t, rmat, inner, outer, half_lhs, send, recv, diag_send, diag_recv, side_ref,
    load_sem, init_sem, out_sem, send_sem, recv_sem, diag_send_sem, diag_recv_sem,
    pass_send_sem, pass_recv_sem, slice_send_sem, slice_recv_sem, stream_send_sem, stream_recv_sem,
    ring_send_sem, ring_recv_sem, ready_sem, go_sem, clear_sem,
):
    nch = vecs.shape[0]
    rows = rmat.shape[1]
    rest = rows - MAIN
    tall = rows // 2
    half = nch // 2
    tile = rows * SIDE
    win = 2 * rows
    f32, bf16 = jnp.float32, jnp.bfloat16

    section = lax.axis_index("section")
    me = lax.axis_index("mat")
    y, z = me // SIDE, me % SIDE
    odd = me % 2
    y_order = [(y + 2) % SIDE, SIDE - 1 - y, y + 1 - 2 * (y % 2), y]
    even_section = section % 2 == 0
    flipped = even_section & (section >= 2)
    last = sections - 1
    f_dot = functools.partial(jnp.dot, preferred_element_type=f32)

    def load(h, space):
        part = pl.ds(h * half, half)
        return pltpu.make_async_copy(eig_ref.at[0, part], space.at[part], load_sem.at[h])

    def load_too(h):
        part = pl.ds(h * half, half)
        return pltpu.make_async_copy(eig_ref.at[0, part], vecs.at[part], load_sem.at[2 + h])

    @pl.when(even_section)
    def _():
        for h in range(2):
            load(h, vecs).start()

    @pl.when(section % 2 == 1)
    def _():
        for h in range(2):
            load(h, vecs_t).start()

    @pl.when(section == 1)
    def _():
        for h in range(2):
            load_too(h).start()

    def row_copies(slot):
        first = pl.multiple_of(odd * rest, rest)
        second = pl.multiple_of(MAIN * (1 - odd), rest)
        return ((pl.ds(first, MAIN), pl.ds(0, MAIN)), (pl.ds(second, rest), pl.ds(MAIN, rest)))

    def init_copies(slot):
        return [
            pltpu.make_async_copy(init_ref.at[slot, a], outer.at[slot, b], init_sem.at[slot, n])
            for n, (a, b) in enumerate(row_copies(slot))
        ]

    def out_copies(slot):
        return [
            pltpu.make_async_copy(rmat.at[slot, b], out_ref.at[0, slot, a], out_sem.at[slot, n])
            for n, (a, b) in enumerate(row_copies(slot))
        ]

    @pl.when(section == 0)
    def _():
        for slot in range(2):
            for copy in init_copies(slot):
                copy.start()

    barrier = pltpu.get_barrier_semaphore()

    @pl.loop(0, MATS)
    def _(peer):
        @pl.when(peer != me)
        def _():
            pl.semaphore_signal(barrier, inc=1, device_id=(section, peer), device_id_type=MESH)

    @pl.when(section > 0)
    def _():
        pl.semaphore_signal(barrier, inc=1, device_id=(section - 1, me), device_id_type=MESH)

    @pl.when(section < sections - 1)
    def _():
        pl.semaphore_signal(barrier, inc=1, device_id=(section + 1, me), device_id_type=MESH)

    has_last = (section + sections - 1) // sections
    has_next = (2 * sections - 2 - section) // sections
    pl.semaphore_wait(barrier, MATS - 1 + has_last + has_next)

    lane = lax.broadcasted_iota(jnp.int32, (tall, MAIN), 1)
    low = lane < rest
    row_id = lax.broadcasted_iota(jnp.int32, (rows, win), 0)
    col_id = lax.broadcasted_iota(jnp.int32, (rows, win), 1)
    target = jnp.where(odd == 0, row_id, jnp.where(row_id < MAIN, row_id + win - MAIN, row_id + rest))
    on_diag = col_id == target
    win_cols = pl.ds(pl.multiple_of((me // 2) * win, MAIN), win)

    def transpose_rows(first, count):
        @pl.loop(first, first + count)
        def _(r):
            part = pl.ds(pl.multiple_of(r * MAIN, MAIN), MAIN)
            vecs_t[:, part] = vecs[part, :].T

    def transpose_in_place(block=256):
        @pl.loop(0, nch // block)
        def _(i):
            @pl.loop(i, nch // block)
            def _(j):
                a = pl.ds(pl.multiple_of(i * block, block), block)
                b = pl.ds(pl.multiple_of(j * block, block), block)
                upper = vecs_t[a, b].T
                lower = vecs_t[b, a].T
                vecs_t[b, a] = upper
                vecs_t[a, b] = lower

    def slice_copy():
        return pltpu.make_async_remote_copy(
            src_ref=outer.at[odd], dst_ref=outer.at[0],
            send_sem=slice_send_sem, recv_sem=slice_recv_sem,
            device_id=(section + 1, me), device_id_type=MESH,
        )

    def slice_arrival():
        return pltpu.make_async_remote_copy(
            src_ref=outer.at[0], dst_ref=outer.at[0],
            send_sem=slice_send_sem, recv_sem=slice_recv_sem,
            device_id=(section - 1, me), device_id_type=MESH,
        )

    def stream_rows(q):
        return pl.ds(pl.multiple_of(q * win, MAIN), win)

    def stream_copy(q):
        return pltpu.make_async_remote_copy(
            src_ref=vecs_t.at[stream_rows(q)], dst_ref=vecs.at[stream_rows(q)],
            send_sem=stream_send_sem.at[q], recv_sem=stream_recv_sem.at[q],
            device_id=(section + 1, me), device_id_type=MESH,
        )

    def stream_arrival(q):
        return pltpu.make_async_remote_copy(
            src_ref=vecs.at[stream_rows(q)], dst_ref=vecs.at[stream_rows(q)],
            send_sem=stream_send_sem.at[q], recv_sem=stream_recv_sem.at[q],
            device_id=(section - 1, me), device_id_type=MESH,
        )

    chunks = nch // win

    def prepare_odd():
        for h in range(2):
            load(h, vecs_t).wait()

        @pl.when(section < last)
        def _():
            @pl.loop(0, nch // MAIN)
            def _(r):
                part = pl.ds(pl.multiple_of(r * MAIN, MAIN), MAIN)
                turned = vecs_t[part, win_cols].T
                outer[0, :, part] = turned[:rows]
                outer[1, :, part] = turned[rows:]
            slice_copy().start()
            slice_copy().wait_send()

        @pl.when(section == 1)
        def _():
            for h in range(2):
                load_too(h).wait()

        @pl.when(section > 1)
        def _():
            @pl.loop(0, chunks)
            def _(q):
                stream_arrival(q).wait_recv()
                outer[0] = vecs[pl.ds(pl.multiple_of(q * win, MAIN), rows), :]
                outer[1] = vecs[pl.ds(pl.multiple_of(q * win + rows, rest), rows), :]
                for n in range(SIDE):
                    cols = slice(n * tile, (n + 1) * tile)
                    block = f_dot(outer[...].reshape(win, nch), vecs_t[:, cols])
                    vecs[stream_rows(q), cols] = block.astype(bf16)
        transpose_in_place()

    def near(axis, step):
        if axis == 0:
            return ((y + step + SIDE) % SIDE) * SIDE + z
        return y * SIDE + (z + step + SIDE) % SIDE

    def ring_block(part, group, step):
        first, second = 1 - part, part
        shift = {first: 0, second: 0}
        if group == 0:
            shift[first] = step
        else:
            shift[first] = group - 1
            shift[second] = step
        return ((y + shift[0] + SIDE) % SIDE) * SIDE + (z + shift[1] + SIDE) % SIDE

    def ring_copy(part, group, kind, arriving=False):
        axis = (1 - part) if group == 0 else part
        origin = (0, 0, -1, 1)[kind]
        if arriving:
            origin = (-1, 1, -2, 2)[kind]
        direction = (1, -1, 1, -1)[kind]
        start = ring_block(part, group, origin) * rows + (tall if kind == 3 else 0)
        size = rows if kind < 2 else tall
        region = vecs.at[pl.ds(pl.multiple_of(start, 32), size), pl.ds(part * half, half)]
        return pltpu.make_async_remote_copy(
            src_ref=region, dst_ref=region,
            send_sem=ring_send_sem.at[part, group, kind],
            recv_sem=ring_recv_sem.at[part, group, kind],
            device_id=(section, near(axis, -direction if arriving else direction)),
            device_id_type=MESH,
        )

    def ring_pass(part, group):
        ring_copy(part, group, 0, True).wait_recv()
        ring_copy(part, group, 2).start()
        ring_copy(part, group, 1, True).wait_recv()
        ring_copy(part, group, 3).start()

    def prepare_even():
        @pl.when(section == 0)
        def _():
            for slot in range(2):
                for copy in init_copies(slot):
                    copy.wait()
            for slot in range(2):
                rmat[slot] = jnp.where(order_ref[slot] == 0, outer[0], outer[1])

        for h in range(2):
            load(h, vecs).wait()

        @pl.when(section > 0)
        def _():
            transpose_rows(0, nch // MAIN)

            @pl.loop(0, chunks)
            def _(q):
                stream_copy(q).start()

            slice_arrival().wait_recv()
            for n in range(SIDE):
                cols = slice(n * tile, (n + 1) * tile)
                outer[1, :, cols] = f_dot(outer[0], vecs[:, cols]).astype(bf16)
            for axis in range(2):
                for step in (1, -1):
                    pl.semaphore_signal(
                        ready_sem, inc=1, device_id=(section, near(axis, step)), device_id_type=MESH
                    )
            vecs[pl.ds(pl.multiple_of(me * rows, rest), rows), :] = outer[1]
            pl.semaphore_wait(ready_sem, 4)
            for part in range(2):
                for group in range(2):
                    for kind in range(2):
                        ring_copy(part, group, kind).start()
            for part in range(2):
                ring_pass(part, 0)
            for part in range(2):
                for group in (2, 4):
                    for kind in range(2):
                        ring_copy(part, group, kind).start()
            for part in range(2):
                ring_pass(part, 1)
            for part in range(2):
                for kind in (2, 3):
                    ring_copy(part, 0, kind, True).wait_recv()
                for kind in range(2):
                    ring_copy(part, 3, kind).start()
            for group in (2, 4, 3):
                for part in range(2):
                    ring_pass(part, group)
            for group in range(1, 5):
                for part in range(2):
                    for kind in (2, 3):
                        ring_copy(part, group, kind, True).wait_recv()
            for part in range(2):
                for group in range(5):
                    for kind in range(4):
                        ring_copy(part, group, kind).wait_send()

            @pl.loop(0, chunks)
            def _(q):
                stream_copy(q).wait_send()

    def block_copy(trip, slot, place, dest):
        return pltpu.make_async_remote_copy(
            src_ref=send.at[slot, place],
            dst_ref=recv.at[trip, slot, me],
            send_sem=send_sem.at[slot, place],
            recv_sem=recv_sem.at[trip, slot, me],
            device_id=(section, dest),
            device_id_type=MESH,
        )

    def block_arrival(trip, slot, source):
        return pltpu.make_async_remote_copy(
            src_ref=send.at[slot, 0],
            dst_ref=recv.at[trip, slot, source],
            send_sem=send_sem.at[slot, 0],
            recv_sem=recv_sem.at[trip, slot, source],
            device_id=(section, source),
            device_id_type=MESH,
        )

    def ship(trip, slot, step, value):
        main_t = value[:MAIN].astype(bf16).T
        rest_t = value[rest:].T
        for j in range(SIDE):
            base = rows * j
            if j % 2 == 0:
                main = main_t[base:base + rows]
                top = rest_t[base:base + tall]
                bottom = rest_t[base + tall:base + rows]
            else:
                main = jnp.concatenate([main_t[base + rest:base + rows], main_t[base:base + rest]], 0)
                top = rest_t[base + rest:base + rest + tall]
                bottom = jnp.concatenate([rest_t[base + rest + tall:base + rows], rest_t[base:base + rest]], 0)
            packed = jnp.where(low, pltpu.roll(top, rest, 1), bottom)
            place = SIDE * step + j
            send[slot, place, :rows] = main
            send[slot, place, rows:] = packed.astype(bf16)
        for j in range(SIDE):
            place = SIDE * step + j
            dest = y_order[step] * SIDE + j
            if step < SIDE - 1:
                block_copy(trip, slot, place, dest).start()
            else:
                @pl.when(j != z)
                def _():
                    block_copy(trip, slot, place, dest).start()
        if step == SIDE - 1:
            recv[trip, slot, me] = send[slot, SIDE * step + z]

    def tile_cols(step):
        return pl.ds(pl.multiple_of(y_order[step] * tile, MAIN), tile)

    def ship_all(trip, slot, product):
        value = product(0)
        for step in range(SIDE):
            after = product(step + 1) if step < SIDE - 1 else None
            ship(trip, slot, step, value)
            value = after

    def wait_sent(trip, slot):
        for place in range(MATS):
            dest = y_order[place // SIDE] * SIDE + place % SIDE
            if place < MATS - SIDE:
                block_copy(trip, slot, place, dest).wait_send()
            else:
                @pl.when(place % SIDE != z)
                def _():
                    block_copy(trip, slot, place, dest).wait_send()

    def gather_group(trip, slot, group, own):
        for n in range(SIDE):
            source = group * SIDE + n
            if own:
                @pl.when(source != me)
                def _():
                    block_arrival(trip, slot, source).wait_recv()
            else:
                block_arrival(trip, slot, source).wait_recv()
        for q in range(SIDE // 2):
            even = group * SIDE + 2 * q
            at = pl.multiple_of(group * tile + win * q, MAIN)
            half_lhs[:, pl.ds(at, MAIN)] = recv[trip, slot, even, :rows]
            half_lhs[:, pl.ds(at + 2 * MAIN, MAIN)] = recv[trip, slot, even + 1, :rows]
            left = recv[trip, slot, even, rows:].astype(f32)
            right = recv[trip, slot, even + 1, rows:].astype(f32)
            top = jnp.where(low, left, pltpu.roll(right, rest, 1))
            bottom = jnp.where(low, pltpu.roll(left, rest, 1), right)
            half_lhs[:tall, pl.ds(at + MAIN, MAIN)] = top.astype(bf16)
            half_lhs[tall:, pl.ds(at + MAIN, MAIN)] = bottom.astype(bf16)

    def gather(trip, slot):
        for step in range(SIDE):
            gather_group(trip, slot, y_order[step], step == SIDE - 1)

    def dot(a, b):
        return jnp.dot(a, b, preferred_element_type=f32)

    def pass_copy(slot, n, source):
        part = pl.ds(n * tile, tile)
        return pltpu.make_async_remote_copy(
            src_ref=source.at[slot, :, part],
            dst_ref=rmat.at[slot, :, part],
            send_sem=pass_send_sem.at[slot, n],
            recv_sem=pass_recv_sem.at[slot, n],
            device_id=(section + 1, me),
            device_id_type=MESH,
        )

    def pass_arrival(slot, n):
        part = pl.ds(n * tile, tile)
        return pltpu.make_async_remote_copy(
            src_ref=rmat.at[slot, :, part],
            dst_ref=rmat.at[slot, :, part],
            send_sem=pass_send_sem.at[slot, n],
            recv_sem=pass_recv_sem.at[slot, n],
            device_id=(section - 1, me),
            device_id_type=MESH,
        )

    def left_half(slot):
        @pl.when(flipped & (slot == 1))
        def _():
            pl.semaphore_wait(clear_sem, 1)

        @pl.when(section > 0)
        def _():
            for n in range(SIDE):
                pass_arrival(slot, n).wait_recv()

        def product(step):
            return dot(rmat[slot], vecs[:, tile_cols(step)])

        ship_all(0, slot, product)

    def diag_copy(slot, dest):
        return pltpu.make_async_remote_copy(
            src_ref=diag_send.at[slot],
            dst_ref=diag_recv.at[slot, me],
            send_sem=diag_send_sem.at[slot, dest],
            recv_sem=diag_recv_sem.at[slot, me],
            device_id=(section, dest),
            device_id_type=MESH,
        )

    def diag_arrival(slot, source):
        return pltpu.make_async_remote_copy(
            src_ref=diag_send.at[slot],
            dst_ref=diag_recv.at[slot, source],
            send_sem=diag_send_sem.at[slot, source],
            recv_sem=diag_recv_sem.at[slot, source],
            device_id=(section, source),
            device_id_type=MESH,
        )

    def inner_product(slot):
        gather(0, slot)

        @pl.when((section % 2 == 1) & (section > 1) & (slot == 0))
        def _():
            pl.semaphore_signal(clear_sem, inc=1, device_id=(section - 1, me), device_id_type=MESH)

        def finish(step):
            cols = tile_cols(step)
            inner[slot, :, cols] = dot(half_lhs[...], vecs[:, cols])

        finish(SIDE - 1)
        mine = jnp.sum(jnp.where(on_diag, inner[slot, :, win_cols], 0.0), axis=0, keepdims=True)
        diag_send[slot] = jnp.zeros(diag_send.shape[1:], f32)
        for n in range(win // MAIN):
            diag_send[slot, n:n + 1, :] = mine[:, n * MAIN:(n + 1) * MAIN]
        diag_recv[slot, me] = diag_send[slot]

        @pl.loop(0, MATS)
        def _(dest):
            @pl.when(dest != me)
            def _():
                diag_copy(slot, dest).start()

        for step in range(SIDE - 1):
            finish(step)

    def propagate(slot):
        @pl.loop(0, MATS)
        def _(source):
            @pl.when(source != me)
            def _():
                diag_arrival(slot, source).wait_recv()

        pieces = []
        for p in range(MATS // 2):
            pair = diag_recv[slot, 2 * p] + diag_recv[slot, 2 * p + 1]
            pieces += [pair[n:n + 1, :] for n in range(win // MAIN)]
        full_diag = jnp.concatenate(pieces, axis=1)
        g_one = g_one_ref[pl.ds(slot, 1), :]
        g_two = g_two_ref[pl.ds(slot, 1), :]
        precond = 1.0 / (g_one + jnp.abs(full_diag))
        side = g_two * precond
        term = g_one - 2.0 * g_two * g_two * precond + g_one * side * side
        side_ref[0:1, :] = side
        side_ref[1:2, :] = term
        side_win = side_ref[0:1, win_cols]
        term_win = side_ref[1:2, win_cols]
        side_rows = jnp.sum(jnp.where(on_diag, side_win, 0.0), axis=1, keepdims=True)
        scaled = side_rows * inner[slot, :, win_cols] * side_win
        outer[slot, :, win_cols] = (scaled + jnp.where(on_diag, term_win, 0.0)).astype(bf16)
        for q in range(nch // win):
            cols = slice(q * win, (q + 1) * win)

            @pl.when(q != me // 2)
            def _():
                outer[slot, :, cols] = (side_rows * inner[slot, :, cols] * side[:, cols]).astype(bf16)

            if q % 2 == 1:
                @pl.when((section > 0) & (section < last))
                def _():
                    pass_copy(slot, q // 2, outer).start()

        @pl.when((section % 2 == 1) & (section > 1) & (section < last) & (slot == 1))
        def _():
            pl.semaphore_signal(go_sem, inc=1, device_id=(section - 1, me), device_id_type=MESH)

    def flip_out(slot):
        @pl.when((slot == 0) & (section < last - 1))
        def _():
            pl.semaphore_wait(go_sem, 1)

        for n in range(SIDE):
            pass_copy(slot, n, outer).wait_send()
        wait_sent(0, slot)
        ship_all(2, slot, lambda step: outer[slot, :, tile_cols(step)].astype(f32))

    def flip_in(slot):
        gather(2, slot)
        outer[slot] = half_lhs[...]

    def right_half(slot):
        wait_sent(1, slot)
        ship_all(1, slot, lambda step: dot(outer[slot], vecs_t[:, tile_cols(step)]))

    def next_rows(slot):
        gather(1, slot)
        for n in range(SIDE):
            cols = slice(n * tile, (n + 1) * tile)
            value = dot(half_lhs[...], vecs_t[:, cols])
            rmat[slot, :, cols] = value.astype(bf16)

            @pl.when(section == 0)
            def _():
                pass_copy(slot, n, rmat).start()
        for copy in out_copies(slot):
            copy.start()

    @pl.when(even_section)
    def _():
        prepare_even()

    @pl.when(section % 2 == 1)
    def _():
        prepare_odd()

    def turn(part):
        transpose_rows(part * (nch // MAIN // 2), nch // MAIN // 2)

    stages = [left_half, inner_product, propagate, right_half, next_rows, flip_out, flip_in, turn]
    is_first = 1 - (section + last) // sections
    is_last = section // last
    is_flipped = (1 - section % 2) * (1 - is_first)
    is_plain = 1 - is_first - is_last - is_flipped
    now, later = (
        is_first * a + is_last * b + is_flipped * c + is_plain * d
        for a, b, c, d in zip(*(digits(order) for order in (FIRST, LAST, FLIPPED, PLAIN)))
    )

    def step(_, queue):
        now, later = queue
        code = now % BASE
        stage, slot = code // 2, code % 2
        for n, run in enumerate(stages):
            @pl.when(stage == n)
            def _():
                run(slot)
        return now // BASE + (later % BASE) * BASE ** (DIGITS - 1), later // BASE

    lax.fori_loop(0, STEPS, step, (now, later))

    @pl.loop(0, 2)
    def _(slot):
        wait_sent(1, slot)
        for copy in out_copies(slot):
            copy.wait()

        @pl.loop(0, MATS)
        def _(dest):
            @pl.when(dest != me)
            def _():
                diag_copy(slot, dest).wait_send()

        @pl.when((section < last) & jnp.logical_not(flipped))
        def _():
            for n in range(SIDE):
                pass_copy(slot, n, rmat).wait_send()


def on_device(sections, eigvec, eig_level, energies, order, init_r):
    nch = eigvec.shape[1]
    rows = init_r.shape[1]
    taken = jnp.where(order == 0, energies[0], energies[1])
    g_one, g_two = greens(eig_level[0][None, :], taken[:, None])
    any_spec = pl.BlockSpec(memory_space=pl.ANY)
    vmem_spec = pl.BlockSpec(memory_space=pltpu.VMEM)
    dma = pltpu.SemaphoreType.DMA
    bf16, f32 = jnp.bfloat16, jnp.float32
    block = rows + rows // 2
    return pl.pallas_call(
        functools.partial(kernel, sections),
        out_shape=jax.ShapeDtypeStruct((1, 2, rows, nch), bf16),
        in_specs=[any_spec, vmem_spec, vmem_spec, any_spec, pl.BlockSpec(memory_space=pltpu.SMEM)],
        out_specs=any_spec,
        scratch_shapes=[
            pltpu.VMEM((nch, nch), bf16),
            pltpu.VMEM((nch, nch), bf16),
            pltpu.VMEM((2, rows, nch), bf16),
            pltpu.VMEM((2, rows, nch), f32),
            pltpu.VMEM((2, rows, nch), bf16),
            pltpu.VMEM((rows, nch), bf16),
            pltpu.VMEM((2, MATS, block, MAIN), bf16),
            pltpu.VMEM((3, 2, MATS, block, MAIN), bf16),
            pltpu.VMEM((2, 8, MAIN), f32),
            pltpu.VMEM((2, MATS, 8, MAIN), f32),
            pltpu.VMEM((2, nch), f32),
            dma((4,)),
            dma((2, 2)),
            dma((2, 2)),
            dma((2, MATS)),
            dma((3, 2, MATS)),
            dma((2, MATS)),
            dma((2, MATS)),
            dma((2, SIDE)),
            dma((2, SIDE)),
            dma(()),
            dma(()),
            dma((nch // (2 * rows),)),
            dma((nch // (2 * rows),)),
            dma((2, 5, SIDE)),
            dma((2, 5, SIDE)),
            pltpu.SemaphoreType.REGULAR,
            pltpu.SemaphoreType.REGULAR,
            pltpu.SemaphoreType.REGULAR,
        ],
        compiler_params=pltpu.CompilerParams(
            collective_id=0, has_side_effects=True, vmem_limit_bytes=67043328
        ),
        name="sectors",
    )(eigvec, g_one, g_two, init_r, order)


def solution(mesh):
    in_specs = (P("section", None, None), P("section", None), P(), P(), P(None, "mat", None))
    out_specs = P("section", None, "mat", None)
    return jax.shard_map(
        functools.partial(on_device, mesh.shape["section"]),
        mesh=mesh, in_specs=in_specs, out_specs=out_specs, check_vma=False,
    )
```
